32 devices in a mesh: px: 8 (over z, y), py: 4 (over x, core).
Axes of the slice: x: 2, y: 2, z: 4, core: 2. Of those that a mesh axis runs over, the one named last changes fastest.
Arguments:
- dofs: float32 [9, 20, 12288], P(None, None, ('px', 'py')), may hold values from -6 to 6
- star: float32 [3, 9, 9, 12288], P(None, None, None, ('px', 'py')), may hold values from -1.25 to 1.25
- flux_minus: float32 [4, 9, 9, 12288], P(None, None, None, ('px', 'py')), may hold values from -2 to 2
- flux_plus: float32 [4, 9, 9, 12288], P(None, None, None, ('px', 'py')), may hold values from -2 to 2
- stiffness: float32 [3, 20, 20], replicated, may hold values from -1.25 to 1.25
- project: float32 [4, 10, 20], replicated, may hold values from -1.25 to 1.25
- lift: float32 [4, 20, 10], replicated, may hold values from -1 to 1
- cluster: int32 [12288], P(('px', 'py')), may hold values from 0 to 1, as said below
- neighbour: int32 [4, 12288], P(None, ('px', 'py')), may hold values from 0 to 767
- neighbour_face: int32 [4, 12288], P(None, ('px', 'py')), may hold values from 0 to 3
- face_type: int32 [4, 12288], P(None, ('px', 'py')), may hold values from 0 to 2, as said below
- send_list: int32 [4, 3072], P(None, ('px', 'py')), may hold values from 0 to 383
Outputs:
- new_dofs: float32 [9, 20, 12288], P(None, None, ('px', 'py'))
The draws below stay inside these ranges and needn't reach their ends.
Inputs may be any that keep to these rules, and one draw needn't show every extreme that they name: 0 is the fast cluster (two substeps of h), 1 the slow one (one step of 2 h); at most 192 of a partition's 384 elements are in cluster 0, and some partition has exactly 192. `neighbour`: below 384: a local element; from 384 on: a ghost in the order of the statement. Used only on faces of type 0. `face_type`: 0 an interior face, 1 a free surface, 2 an absorbing face. `send_list`: local element indices of the partition.
All inputs are finite; a program needn't handle non-finite values.
Results may differ from the reference program's by a relative error of at most 0.0003.
Values sent between devices are 32-bit elements; how exact they have to be, the bound alone decides.
No kernel may reach another device: no remote copies, remote signals or barrier semaphores. Data moves between devices by JAX's collectives and lax.ppermute only.
A program may use at most 64 MiB of HBM per device.

```python
import jax
import jax.numpy as jnp
from jax import lax

Q = 9
B = 20
FB = 10
NE_DEV = 384
SEND = 96
FAST_MAX = 192
NE_TOTAL = 12288
SEND_TOTAL = 3072
N_PX = 8
N_PY = 4


def draw_cluster(key, part):
    groups = NE_TOTAL // NE_DEV
    first_key, second_key, third_key = jax.random.split(key, 3)
    counts = jax.random.randint(first_key, (groups,), NE_DEV // 8, FAST_MAX + 1)
    busiest = jax.random.randint(second_key, (), 0, groups)
    counts = jnp.where(jnp.arange(groups) == busiest, FAST_MAX, counts)
    subkeys = jax.random.split(third_key, groups)

    def one_order(single_key):
        return jax.random.permutation(single_key, NE_DEV)
    orders = jax.vmap(one_order)(subkeys)
    labels = jnp.where(orders < counts[:, None], 0, 1)
    return labels.reshape(-1).astype(jnp.int32)


def draw_face_type(key, part):
    rolled = jax.random.randint(key, (4, NE_TOTAL), 0, 16)
    kinds = jnp.where(rolled == 15, 2, jnp.where(rolled == 14, 1, 0))
    return kinds.astype(jnp.int32)


def touch_ends(values, own_key, least, largest):
    longest = values.shape.index(max(values.shape))
    spots = []
    for shift in (0, 1):
        where = [jax.random.randint(jax.random.fold_in(own_key, axis), (), 0, length) for axis, length in enumerate(values.shape)]
        where[longest] = (where[longest] + shift) % values.shape[longest]
        spots.append(tuple(where))
    return values.at[spots[0]].set(least).at[spots[1]].set(largest)


def block_levels(key, dims, cuts, smallest, high):
    loudness = 1.0
    for position, blocks in cuts:
        steps = jax.random.uniform(jax.random.fold_in(jax.random.fold_in(key, 6), position), (blocks,), jnp.float32, smallest / len(cuts), high / len(cuts))
        loudness = loudness * jnp.repeat(jnp.exp(steps), dims[position] // blocks).reshape((-1,) + (1,) * (len(dims) - 1 - position))
    return loudness


def gaussian(own_key, shape, scale, bound, shards=(), held_as=jnp.bfloat16):
    loudness = block_levels(own_key, shape, shards, -0.22, 0.18) if shards else 1.0
    values = jax.random.normal(own_key, shape, jnp.float32) * scale * loudness
    return jnp.minimum(jnp.maximum(values, -bound), bound).astype(held_as)


def setup_inputs(seed: int = 0) -> dict:
    splits = jax.random.split(jax.random.key(seed), 13)
    return {
        "dofs": gaussian(splits[0], (Q, B, NE_TOTAL), 1.0, 6.0, ((2, 32),), jnp.float32),
        "star": gaussian(splits[1], (3, Q, Q, NE_TOTAL), (3 * Q) ** -0.5, 1.25, ((3, 32),), jnp.float32),
        "flux_minus": gaussian(splits[2], (4, Q, Q, NE_TOTAL), Q ** -0.5, 2.0, ((3, 32),), jnp.float32),
        "flux_plus": gaussian(splits[3], (4, Q, Q, NE_TOTAL), Q ** -0.5, 2.0, ((3, 32),), jnp.float32),
        "stiffness": gaussian(splits[4], (3, B, B), B ** -0.5, 1.25, (), jnp.float32),
        "project": gaussian(splits[5], (4, FB, B), B ** -0.5, 1.25, (), jnp.float32),
        "lift": gaussian(splits[6], (4, B, FB), (4 * FB) ** -0.5, 1.0, (), jnp.float32),
        "cluster": draw_cluster(jax.random.fold_in(splits[12], 71), 0),
        "neighbour": touch_ends(jax.random.randint(splits[8], (4, NE_TOTAL), 0, NE_DEV + 4 * SEND), jax.random.fold_in(splits[8], 1), 0, (NE_DEV + 4 * SEND) - 1).astype(jnp.int32),
        "neighbour_face": touch_ends(jax.random.randint(splits[9], (4, NE_TOTAL), 0, 4), jax.random.fold_in(splits[9], 1), 0, 3).astype(jnp.int32),
        "face_type": draw_face_type(jax.random.fold_in(splits[12], 71), 0),
        "send_list": touch_ends(jax.random.randint(splits[11], (4, SEND_TOTAL), 0, NE_DEV), jax.random.fold_in(splits[11], 1), 0, NE_DEV - 1).astype(jnp.int32),
    }


highest = lax.Precision.HIGHEST
step_length = 0.5
factorials = (1.0, 2.0, 6.0, 24.0)


def basis_apply(matrix, field):
    return jnp.einsum('jk,qke->qje', matrix, field, precision=highest)


def element_mix(matrix, field):
    total = matrix[:, 0, None, :] * field[0][None, :, :]
    for inner in range(1, field.shape[0]):
        total = total + matrix[:, inner, None, :] * field[inner][None, :, :]
    return total


def derivatives(field, star, stiffness):
    series = [field]
    for degree in range(3):
        current = series[-1]
        following = element_mix(star[0], basis_apply(stiffness[0], current))
        for column in (1, 2):
            following = following + element_mix(star[column], basis_apply(stiffness[column], current))
        series.append(-following)
    return series


def integrate(series, lower_time, upper_time):
    summed = jnp.zeros_like(series[0])
    for degree in range(4):
        weight = (upper_time ** (degree + 1) - lower_time ** (degree + 1)) / factorials[degree]
        summed = summed + weight * series[degree]
    return summed


def update(own, extended, star, minus, plus, neighbour, neighbour_face, face_type, stiffness, project, lift):
    result = basis_apply(stiffness[0].T, element_mix(star[0], own))
    for column in (1, 2):
        result = result + basis_apply(stiffness[column].T, element_mix(star[column], own))
    traces = jnp.stack([basis_apply(project[which], extended) for which in range(4)])
    for which_face in range(4):
        own_trace = basis_apply(project[which_face], own)
        result = result - basis_apply(lift[which_face], element_mix(minus[which_face], own_trace))
        picked = jnp.take(traces, neighbour[which_face], axis=3)
        choose = (neighbour_face[which_face][None, :] == jnp.arange(4)[:, None]).astype(jnp.float32)
        across = jnp.sum(picked * choose[:, None, None, :], axis=0)
        face_kind = face_type[which_face]
        across = jnp.where(face_kind == 0, across, jnp.where(face_kind == 1, own_trace, 0.0))
        result = result - basis_apply(lift[which_face], element_mix(plus[which_face], across))
    return result


def shift_grid(values, axis, amount):
    length = values.shape[axis]
    blank_row = jnp.zeros_like(lax.slice_in_dim(values, 0, 1, axis=axis))
    if amount > 0:
        return jnp.concatenate([blank_row, lax.slice_in_dim(values, 0, length - 1, axis=axis)], axis=axis)
    return jnp.concatenate([lax.slice_in_dim(values, 1, length, axis=axis), blank_row], axis=axis)


def reference(dofs, star, flux_minus, flux_plus, stiffness, project, lift, cluster, neighbour, neighbour_face, face_type, send_list):
    blocks = N_PX * N_PY

    def split_blocks(array, width_each):
        return jnp.moveaxis(array.reshape(array.shape[:-1] + (blocks, width_each)), -2, 0)

    part_dofs = split_blocks(dofs, NE_DEV)
    part_star = split_blocks(star, NE_DEV)
    part_minus = split_blocks(flux_minus, NE_DEV)
    part_plus = split_blocks(flux_plus, NE_DEV)
    part_cluster = split_blocks(cluster, NE_DEV)
    part_neighbour = split_blocks(neighbour, NE_DEV)
    part_face = split_blocks(neighbour_face, NE_DEV)
    part_type = split_blocks(face_type, NE_DEV)
    part_send = split_blocks(send_list, SEND)

    def ghosts_of(buffers):
        def pick_rows(buffer, rows):
            return buffer[:, :, rows]

        taken = jax.vmap(pick_rows)(buffers, part_send)
        grid = taken.reshape((N_PX, N_PY) + taken.shape[1:])
        lower_x = shift_grid(grid[:, :, :, :, 1], 0, 1)
        upper_x = shift_grid(grid[:, :, :, :, 0], 0, -1)
        lower_y = shift_grid(grid[:, :, :, :, 3], 1, 1)
        upper_y = shift_grid(grid[:, :, :, :, 2], 1, -1)
        ghosts = jnp.concatenate([lower_x, upper_x, lower_y, upper_y], axis=-1)
        return ghosts.reshape((blocks,) + ghosts.shape[2:])

    def predict_first(items):
        field, star_part = items
        series = derivatives(field, star_part, stiffness)
        return integrate(series, 0.0, step_length), integrate(series, step_length, 2.0 * step_length)

    first_buf, late_buf = lax.map(predict_first, (part_dofs, part_star))
    extended_first = jnp.concatenate([first_buf, ghosts_of(first_buf)], axis=-1)

    def middle(items):
        field, own, extended, star_part, minus, plus, near, near_face, kinds, labels, late = items
        change = update(own, extended, star_part, minus, plus, near, near_face, kinds, stiffness, project, lift)
        midway = field + change
        fresh = integrate(derivatives(midway, star_part, stiffness), 0.0, step_length)
        return change, jnp.where(labels == 0, fresh, late)

    change_first, second_buf = lax.map(middle, (part_dofs, first_buf, extended_first, part_star, part_minus, part_plus, part_neighbour, part_face, part_type, part_cluster, late_buf))
    extended_second = jnp.concatenate([second_buf, ghosts_of(second_buf)], axis=-1)

    def finish(items):
        field, change, own, extended, star_part, minus, plus, near, near_face, kinds = items
        change_second = update(own, extended, star_part, minus, plus, near, near_face, kinds, stiffness, project, lift)
        return field + change + change_second

    result = lax.map(finish, (part_dofs, change_first, second_buf, extended_second, part_star, part_minus, part_plus, part_neighbour, part_face, part_type))
    result = jnp.moveaxis(result, 0, 2)
    return result.reshape(result.shape[0], result.shape[1], blocks * NE_DEV)
```

```python
import functools
import math

import jax
import jax.numpy as jnp
from jax import lax
from jax.experimental import pallas as pl
from jax.experimental.pallas import tpu as pltpu
from jax.sharding import PartitionSpec as P

f32, bf16 = jnp.float32, jnp.bfloat16
step_length = 0.5
LANES = 128
DIRS = 4


def weights_of(lower, upper):
    return [
        (upper ** (m + 1) - lower ** (m + 1)) / math.factorial(m + 1) for m in range(4)
    ]


def iota(shape, dim):
    return lax.broadcasted_iota(jnp.int32, shape, dim)


def split(x):
    high = x.astype(bf16)
    return high, (x - high.astype(f32)).astype(bf16)


def triple(x):
    high = x.astype(bf16).astype(f32)
    return jnp.concatenate([high, x - high, high], axis=0).astype(bf16)


def pad_rows(x, rows):
    return jnp.concatenate([x, x[2 * x.shape[0] - rows :]], axis=0)


def spread(matrix, rep, transposed):
    dims = (((0,) if transposed else (1,), (0,)), ((), ()))
    high, low = split(matrix)
    return [
        lax.dot_general(part, rep, dims, preferred_element_type=f32)
        for part in (high, low)
    ]


def block_weights(matrix, inner, copies, transposed):
    count = matrix.shape[0] if transposed else matrix.shape[1]
    width = 3 * copies * inner
    rep = (iota((count, width), 1) % inner == iota((count, width), 0)).astype(bf16)
    high, low = spread(matrix, rep, transposed)
    col = iota(high.shape, 1)
    both = jnp.where(col < 2 * copies * inner, high, low)
    owner = (col % (copies * inner)) // inner
    return [jnp.where(owner == q, both, 0.0) for q in range(copies)]


def series_weights(stiff_ref, rows, transposed):
    out = []
    for c in range(3):
        for block in block_weights(stiff_ref[c], rows, 3, transposed):
            out.append(pad_rows(block, rows))
    return jnp.concatenate(out, axis=0).astype(bf16)


def stacked(ref, first, count):
    return jnp.concatenate([ref[first + i] for i in range(count)], axis=0)


def star_mix(star_ref, t_ref, lane, quantities):
    rows = t_ref.shape[1]
    acc = [None] * quantities
    for c in range(3):
        for q in range(quantities):
            t = t_ref[c * quantities + q, :, lane]
            for p in range(quantities):
                term = jnp.broadcast_to(star_ref[p, q, c : c + 1, lane], (rows, LANES)) * t
                acc[p] = term if acc[p] is None else acc[p] + term
    return acc


def lane_tiles(n, body):
    def one(tile, carry):
        body(pl.ds(pl.multiple_of(tile * LANES, LANES), LANES))
        return carry

    lax.fori_loop(0, n // LANES, one, 0)


def stiff_products(w_ref, v_ref, t_ref, quantities):
    rows = v_ref.shape[1]
    for g in range(quantities // 3):
        x = triple(stacked(v_ref, 3 * g, 3))
        t = jnp.dot(w_ref[...], x, preferred_element_type=f32)
        for c in range(3):
            for i in range(3):
                start = (3 * c + i) * rows
                t_ref[c * quantities + 3 * g + i] = t[start : start + rows]


def series(w_ref, v_ref, t_ref, star_ref, sums):
    quantities = v_ref.shape[0]
    for ref, weights in sums:
        for q in range(quantities):
            ref[q] = weights[0] * v_ref[q]
    for m in range(1, 4):
        stiff_products(w_ref, v_ref, t_ref, quantities)

        def tile(lane, m=m):
            acc = star_mix(star_ref, t_ref, lane, quantities)
            for p in range(quantities):
                value = -acc[p]
                if m < 3:
                    v_ref[p, :, lane] = value
                for ref, weights in sums:
                    ref[p, :, lane] += weights[m] * value

        lane_tiles(v_ref.shape[2], tile)


def pack_sends(buffer_ref, lists_ref, out_ref, parity):
    quantities, rows, n = buffer_ref.shape
    high, low = split(stacked(buffer_ref, 0, quantities))
    both = jnp.concatenate([high, low], axis=0)
    count = lists_ref.shape[1]
    wanted = lists_ref[...]
    for e in range(DIRS):
        axis = e // 2
        even, odd = (1, 0) if e % 2 == 0 else (0, 1)
        row = jnp.where(
            parity[axis] == 0,
            wanted[2 * axis + even : 2 * axis + even + 1],
            wanted[2 * axis + odd : 2 * axis + odd + 1],
        )
        pick = (iota((n, count), 0) == row).astype(bf16)
        got = jnp.dot(both, pick, preferred_element_type=f32)
        total = got[: quantities * rows] + got[quantities * rows :]
        for q in range(quantities):
            out_ref[e, q] = total[q * rows : (q + 1) * rows]


def parities(axes):
    return [lax.rem(lax.axis_index(axis), 2) for axis in axes]


def predict_kernel(axes, dofs_ref, star_ref, stiff_ref, lists_ref, first_ref, late_ref, send_ref, w_ref, v_ref, t_ref):
    h = step_length
    rows = first_ref.shape[1]
    w_ref[...] = series_weights(stiff_ref, rows, False)
    for q in range(dofs_ref.shape[0]):
        v_ref[q] = pad_rows(dofs_ref[q], rows)
    sums = [(first_ref, weights_of(0.0, h)), (late_ref, weights_of(h, 2 * h))]
    series(w_ref, v_ref, t_ref, star_ref, sums)
    pack_sends(first_ref, lists_ref, send_ref, parities(axes))


def effective(type_ref, near_ref, face_ref):
    kind = type_ref[...]
    n = kind.shape[1]
    index = jnp.where(kind == 0, near_ref[...], jnp.where(kind == 1, iota(kind.shape, 1), -1))
    source = jnp.where(kind == 0, face_ref[...], jnp.where(kind == 1, iota(kind.shape, 0), 0))
    return index, source


def across_weights(project_ref):
    faces_basis, faces, count = project_ref.shape
    main = (count // 8) * 8
    rest = count - main
    width = faces * count
    col = iota((count, 3 * width), 1) % width
    basis = jnp.where(col < faces * main, col % main, main + (col - faces * main) % rest)
    rep = (basis == iota((count, 3 * width), 0)).astype(bf16)
    tall = faces_basis * faces
    grow = (iota((tall, faces_basis), 0) // faces == iota((tall, faces_basis), 1)).astype(bf16)
    col = iota((tall, 3 * width), 1)
    inner = col % width
    owner = jnp.where(inner < faces * main, inner // main, (inner - faces * main) // rest)
    mine = owner == iota((tall, 3 * width), 0) % faces
    out = []
    for g in range(faces):
        matrix = jnp.concatenate([project_ref[b, g : g + 1] for b in range(faces_basis)], axis=0)
        high, low = spread(matrix, rep, False)
        high = jnp.dot(grow, high.astype(bf16), preferred_element_type=f32)
        low = jnp.dot(grow, low.astype(bf16), preferred_element_type=f32)
        out.append(jnp.where(mine, jnp.where(col < 2 * width, high, low), 0.0))
    return jnp.concatenate(out, axis=0).astype(bf16)


def across_operand(picked, q, rows, height):
    parts = []
    for part in range(2):
        start = part * height + q * rows
        main = [ref[start : start + 16] for ref in picked]
        rest = [ref[start + 16 : start + 24] for ref in picked]
        lower = iota(rest[0].shape, 0) < 4
        parts.append(
            jnp.concatenate(
                main + [jnp.where(lower, rest[0], rest[1]), jnp.where(lower, rest[2], rest[3])], axis=0
            )
        )
    return jnp.concatenate([parts[0], parts[1], parts[0]], axis=0).astype(bf16)


def across_traces(w_ref, picked, source, quantities, rows, store):
    height = quantities * rows
    faces = len(picked)
    tall = w_ref.shape[0] // faces
    wide = jnp.concatenate([source] * (tall // faces), axis=0)
    tests = [wide == g for g in range(faces - 1)]
    for q in range(quantities):
        z = jnp.dot(
            w_ref[...], across_operand(picked, q, rows, height), preferred_element_type=f32
        )
        value = z[(faces - 1) * tall :]
        for g in reversed(range(faces - 1)):
            value = jnp.where(tests[g], z[g * tall : (g + 1) * tall], value)
        store(q, value)


def flux_mix(flux_ref, trace_ref, lane, start):
    quantities, tall = trace_ref.shape[0], trace_ref.shape[1]
    faces = flux_ref.shape[2]
    acc = list(start)
    for q in range(quantities):
        t = trace_ref[q, :, lane]
        for p in range(quantities):
            factor = flux_ref[p, q, :, lane]
            term = jnp.concatenate([factor] * (tall // faces), axis=0) * t
            acc[p] = term if acc[p] is None else acc[p] + term
    return acc


def own_kernel(own_ref, star_ref, minus_ref, stiff_ref, project_ref, near_ref, face_ref, type_ref,
               part_ref, g_ref, across_ref, w_ref, wa_ref, trace_ref, t_ref, picked_ref, pick_ref):
    quantities, rows, n = own_ref.shape
    faces_basis, faces, count = project_ref.shape
    tall = faces_basis * faces
    flat = jnp.concatenate([project_ref[b] for b in range(faces_basis)], axis=0)
    w_ref[: 9 * rows] = series_weights(stiff_ref, rows, True)
    w_ref[9 * rows :] = jnp.concatenate(block_weights(flat, rows, 3, False), axis=0).astype(bf16)
    wa_ref[...] = across_weights(project_ref)
    for g in range(quantities // 3):
        x = triple(stacked(own_ref, 3 * g, 3))
        t = jnp.dot(w_ref[...], x, preferred_element_type=f32)
        for c in range(3):
            for i in range(3):
                start = (3 * c + i) * rows
                t_ref[c * quantities + 3 * g + i] = t[start : start + rows]
        for i in range(3):
            start = 9 * rows + i * tall
            trace_ref[3 * g + i] = t[start : start + tall]

    index, source = effective(type_ref, near_ref, face_ref)
    high, low = split(stacked(own_ref, 0, quantities))
    both = jnp.concatenate([high, low], axis=0)
    for f in range(faces):
        pick_ref[...] = (iota((n, n), 0) == index[f : f + 1]).astype(bf16)
        picked_ref[f] = jnp.dot(both, pick_ref[...], preferred_element_type=f32)

    def keep(q, value):
        across_ref[q] = value

    across_traces(wa_ref, [picked_ref.at[f] for f in range(faces)], source, quantities, rows, keep)

    def tile(lane):
        acc = star_mix(star_ref, t_ref, lane, quantities)
        for p in range(quantities):
            part_ref[p, :, lane] = acc[p]
        acc = flux_mix(minus_ref, trace_ref, lane, [None] * quantities)
        for p in range(quantities):
            g_ref[p, :, lane] = acc[p]

    lane_tiles(n, tile)


def lift_weights(lift_ref, rows):
    faces_basis = lift_ref.shape[0]
    flat = jnp.concatenate([lift_ref[b] for b in range(faces_basis)], axis=0)
    blocks = block_weights(flat, flat.shape[0], 2, True)
    return jnp.concatenate([pad_rows(block, rows) for block in blocks], axis=0).astype(bf16)


def ghost_part(axes, got_refs, plus_ref, project_ref, lift_ref, near_ref, face_ref, type_ref,
               part_ref, g_ref, across_ref, wa_ref, wl_ref, picked_ref, pick_ref, trace_ref, flux_ref, emit):
    quantities, rows, n = part_ref.shape
    faces = project_ref.shape[1]
    count = got_refs[0].shape[2]
    wa_ref[...] = across_weights(project_ref)
    wl_ref[...] = lift_weights(lift_ref, rows)
    index, source = effective(type_ref, near_ref, face_ref)
    parity = parities(axes)
    ghost = index - n
    block = ghost // count
    axis_parity = jnp.where(block < 2, parity[0], parity[1])
    slot = (block // 2) * 2 + jnp.where(block % 2 == 1, axis_parity, 1 - axis_parity)
    column = jnp.where(ghost >= 0, slot * LANES + ghost % count, -1)
    operands = []
    for e in range(DIRS):
        high, low = split(stacked(got_refs[e], 0, quantities))
        both = jnp.concatenate([high, low], axis=0)
        empty = jnp.zeros((both.shape[0], LANES - count), bf16)
        operands.append(jnp.concatenate([both, empty], axis=1))
    operand = jnp.concatenate(operands, axis=1)
    for f in range(faces):
        pick_ref[...] = (iota((DIRS * LANES, n), 0) == column[f : f + 1]).astype(bf16)
        picked_ref[f] = jnp.dot(operand, pick_ref[...], preferred_element_type=f32)

    def keep(q, value):
        trace_ref[q] = across_ref[q] + value

    across_traces(wa_ref, [picked_ref.at[f] for f in range(faces)], source, quantities, rows, keep)

    def tile(lane):
        acc = flux_mix(plus_ref, trace_ref, lane, [g_ref[p, :, lane] for p in range(quantities)])
        for p in range(quantities):
            flux_ref[p, :, lane] = acc[p]

    lane_tiles(n, tile)
    for pair in range(0, quantities, 2):
        two = pair + 1 < quantities
        x = jnp.concatenate(
            [flux_ref[pair], flux_ref[pair + 1] if two else jnp.zeros(flux_ref.shape[1:], f32)], axis=0
        )
        lifted = jnp.dot(wl_ref[...], triple(x), preferred_element_type=f32)
        emit(pair, part_ref[pair] - lifted[:rows])
        if two:
            emit(pair + 1, part_ref[pair + 1] - lifted[rows:])


def middle_kernel(axes, got0, got1, got2, got3, plus_ref, project_ref, lift_ref, near_ref, face_ref, type_ref,
                  part_ref, g_ref, across_ref, dofs_ref, star_ref, stiff_ref, cluster_ref, late_ref, lists_ref,
                  midway_ref, second_ref, send_ref,
                  wa_ref, wl_ref, picked_ref, pick_ref, trace_ref, flux_ref, w_ref, v_ref, t_ref):
    rows = part_ref.shape[1]
    quantities = part_ref.shape[0]

    def emit(q, change):
        value = pad_rows(dofs_ref[q], rows) + change
        midway_ref[q] = value
        v_ref[q] = value

    ghost_part(axes, [got0, got1, got2, got3], plus_ref, project_ref, lift_ref, near_ref, face_ref, type_ref,
               part_ref, g_ref, across_ref, wa_ref, wl_ref, picked_ref, pick_ref, trace_ref, flux_ref, emit)
    w_ref[...] = series_weights(stiff_ref, rows, False)
    series(w_ref, v_ref, t_ref, star_ref, [(second_ref, weights_of(0.0, step_length))])
    fast = cluster_ref[...] == 0
    for q in range(quantities):
        second_ref[q] = jnp.where(fast, second_ref[q], late_ref[q])
    pack_sends(second_ref, lists_ref, send_ref, parities(axes))


def finish_kernel(axes, got0, got1, got2, got3, plus_ref, project_ref, lift_ref, near_ref, face_ref, type_ref,
                  part_ref, g_ref, across_ref, midway_ref, out_ref,
                  wa_ref, wl_ref, picked_ref, pick_ref, trace_ref, flux_ref):
    count = out_ref.shape[1]

    def emit(q, change):
        out_ref[q] = (midway_ref[q] + change)[:count]

    ghost_part(axes, [got0, got1, got2, got3], plus_ref, project_ref, lift_ref, near_ref, face_ref, type_ref,
               part_ref, g_ref, across_ref, wa_ref, wl_ref, picked_ref, pick_ref, trace_ref, flux_ref, emit)


def call(kernel, name, args, outs, scratch, flops):
    spec = pl.BlockSpec(memory_space=pltpu.VMEM)
    size = sum(4 * math.prod(a.shape) for a in list(args) + list(outs))
    return pl.pallas_call(
        kernel,
        out_shape=[jax.ShapeDtypeStruct(s.shape, s.dtype) for s in outs],
        in_specs=[spec] * len(args),
        out_specs=[spec] * len(outs),
        scratch_shapes=scratch,
        cost_estimate=pl.CostEstimate(flops=flops, bytes_accessed=size, transcendentals=0),
        name=name,
    )(*args)


def exchange(block, axis, offset):
    count = lax.axis_size(axis)
    route = []
    for i in range(offset, count - 1, 2):
        route += [(i, i + 1), (i + 1, i)]
    return lax.ppermute(block, axis, route)


def swap(sends):
    return [
        exchange(sends[0], "px", 0),
        exchange(sends[1], "px", 1),
        exchange(sends[2], "py", 0),
        exchange(sends[3], "py", 1),
    ]


def per_device(dofs, star, flux_minus, flux_plus, stiffness, project, lift, cluster, neighbour, neighbour_face,
               face_type, send_list):
    axes = ("px", "py")
    quantities, count, n = dofs.shape
    faces, faces_basis = project.shape[:2]
    rows = 8 * pl.cdiv(count, 8)
    tall = faces * faces_basis
    width = send_list.shape[1]
    star = jnp.transpose(star, (1, 2, 0, 3))
    minus = jnp.transpose(flux_minus, (1, 2, 0, 3))
    plus = jnp.transpose(flux_plus, (1, 2, 0, 3))
    project = jnp.transpose(project, (1, 0, 2))
    lift = jnp.transpose(lift, (2, 0, 1))
    cluster = cluster.reshape(1, n)

    field = jax.ShapeDtypeStruct((quantities, rows, n), f32)
    traces = jax.ShapeDtypeStruct((quantities, tall, n), f32)
    sends = jax.ShapeDtypeStruct((DIRS, quantities, rows, width), f32)
    series_w = pltpu.VMEM((9 * rows, 9 * rows), bf16)
    v_field = pltpu.VMEM((quantities, rows, n), f32)
    t_field = pltpu.VMEM((3 * quantities, rows, n), f32)
    t_trace = pltpu.VMEM((quantities, tall, n), f32)
    across_w = pltpu.VMEM((faces * tall, 3 * faces * count), bf16)
    lift_w = pltpu.VMEM((2 * rows, 6 * tall), bf16)
    picked = pltpu.VMEM((faces, 2 * quantities * rows, n), f32)

    first, late, out = call(
        functools.partial(predict_kernel, axes), "predict", (dofs, star, stiffness, send_list),
        (field, field, sends), [series_w, v_field, t_field], 10_000_000)

    def own(buffer, name):
        return call(
            own_kernel, name, (buffer, star, minus, stiffness, project, neighbour, neighbour_face, face_type),
            (field, traces, traces),
            [pltpu.VMEM((9 * rows + 3 * tall, 9 * rows), bf16), across_w, t_trace, t_field, picked,
             pltpu.VMEM((n, n), bf16)], 10_000_000)

    ghost_scratch = [across_w, lift_w, picked, pltpu.VMEM((DIRS * LANES, n), bf16), t_trace, t_trace]
    got = swap([out[e] for e in range(DIRS)])
    part, g, across = own(first, "own_first")
    midway, second, out = call(
        functools.partial(middle_kernel, axes), "middle",
        (*got, plus, project, lift, neighbour, neighbour_face, face_type, part, g, across, dofs, star, stiffness,
         cluster, late, send_list),
        (field, field, sends), ghost_scratch + [series_w, v_field, t_field], 10_000_000)
    got = swap([out[e] for e in range(DIRS)])
    part, g, across = own(second, "own_second")
    (result,) = call(
        functools.partial(finish_kernel, axes), "finish",
        (*got, plus, project, lift, neighbour, neighbour_face, face_type, part, g, across, midway),
        (jax.ShapeDtypeStruct((quantities, count, n), f32),), ghost_scratch, 10_000_000)
    return result


def solution(mesh):
    both = ("px", "py")
    in_specs = (
        P(None, None, both),
        P(None, None, None, both),
        P(None, None, None, both),
        P(None, None, None, both),
        P(),
        P(),
        P(),
        P(both),
        P(None, both),
        P(None, both),
        P(None, both),
        P(None, both),
    )
    return jax.shard_map(
        per_device, mesh=mesh, in_specs=in_specs, out_specs=P(None, None, both), check_vma=False
    )
```

```python
import functools
import math

import jax
import jax.numpy as jnp
from jax import lax
from jax.experimental import pallas as pl
from jax.experimental.pallas import tpu as pltpu
from jax.sharding import PartitionSpec as P

f32, bf16 = jnp.float32, jnp.bfloat16
step_length = 0.5
LANES = 128
DIRS = 4


def weights_of(lower, upper):
    return [
        (upper ** (m + 1) - lower ** (m + 1)) / math.factorial(m + 1) for m in range(4)
    ]


def iota(shape, dim):
    return lax.broadcasted_iota(jnp.int32, shape, dim)


def split(x):
    high = x.astype(bf16)
    return high, (x - high.astype(f32)).astype(bf16)


def triple(x):
    high = x.astype(bf16).astype(f32)
    return jnp.concatenate([high, x - high, high], axis=0).astype(bf16)


def pad_rows(x, rows):
    return jnp.concatenate([x, x[2 * x.shape[0] - rows :]], axis=0)


def spread(matrix, rep, transposed):
    dims = (((0,) if transposed else (1,), (0,)), ((), ()))
    high, low = split(matrix)
    return [
        lax.dot_general(part, rep, dims, preferred_element_type=f32)
        for part in (high, low)
    ]


def block_weights(matrix, inner, copies, transposed):
    count = matrix.shape[0] if transposed else matrix.shape[1]
    width = 3 * copies * inner
    rep = (iota((count, width), 1) % inner == iota((count, width), 0)).astype(bf16)
    high, low = spread(matrix, rep, transposed)
    col = iota(high.shape, 1)
    both = jnp.where(col < 2 * copies * inner, high, low)
    owner = (col % (copies * inner)) // inner
    return [jnp.where(owner == q, both, 0.0) for q in range(copies)]


def series_weights(stiff_ref, rows, transposed):
    out = []
    for c in range(3):
        for block in block_weights(stiff_ref[c], rows, 3, transposed):
            out.append(pad_rows(block, rows))
    return jnp.concatenate(out, axis=0).astype(bf16)


def stacked(ref, first, count):
    return jnp.concatenate([ref[first + i] for i in range(count)], axis=0)


def star_mix(star_ref, t_ref, lane, quantities):
    rows = t_ref.shape[1]
    acc = [None] * quantities
    for c in range(3):
        for q in range(quantities):
            t = t_ref[c * quantities + q, :, lane]
            for p in range(quantities):
                term = jnp.broadcast_to(star_ref[p, q, c : c + 1, lane], (rows, LANES)) * t
                acc[p] = term if acc[p] is None else acc[p] + term
    return acc


def lane_tiles(n, body):
    def one(tile, carry):
        body(pl.ds(pl.multiple_of(tile * LANES, LANES), LANES))
        return carry

    lax.fori_loop(0, n // LANES, one, 0)


def stiff_products(w_ref, v_ref, t_ref, lane):
    quantities, rows = v_ref.shape[:2]
    for g in range(quantities // 3):
        x = jnp.concatenate([v_ref[3 * g + i, :, lane] for i in range(3)], axis=0)
        t = jnp.dot(w_ref[...], triple(x), preferred_element_type=f32)
        for c in range(3):
            for i in range(3):
                start = (3 * c + i) * rows
                t_ref[c * quantities + 3 * g + i, :, lane] = t[start : start + rows]


def series(w_ref, v_ref, t_ref, star_ref, sums):
    quantities, _, n = v_ref.shape
    tiles = n // LANES
    for ref, weights in sums:
        for q in range(quantities):
            ref[q] = weights[0] * v_ref[q]
    stiff_products(w_ref, v_ref, t_ref, pl.ds(0, n))
    for m in range(1, 4):

        def tile(index, carry, m=m):
            lane = pl.ds(pl.multiple_of(index * LANES, LANES), LANES)
            acc = star_mix(star_ref, t_ref, lane, quantities)
            for p in range(quantities):
                value = -acc[p]
                if m < 3:
                    v_ref[p, :, lane] = value
                for ref, weights in sums:
                    ref[p, :, lane] += weights[m] * value
            return carry

        lax.fori_loop(0, tiles, tile, 0)
        if m < 3:
            stiff_products(w_ref, v_ref, t_ref, pl.ds(0, n))


def pack_sends(buffer_ref, lists_ref, out_refs, parity):
    quantities, rows, n = buffer_ref.shape
    high, low = split(stacked(buffer_ref, 0, quantities))
    both = jnp.concatenate([high, low], axis=0)
    count = lists_ref.shape[1]
    wanted = lists_ref[...]
    for e in range(DIRS):
        axis = e // 2
        even, odd = (1, 0) if e % 2 == 0 else (0, 1)
        row = jnp.where(
            parity[axis] == 0,
            wanted[2 * axis + even : 2 * axis + even + 1],
            wanted[2 * axis + odd : 2 * axis + odd + 1],
        )
        pick = (iota((n, count), 0) == row).astype(bf16)
        got = jnp.dot(both, pick, preferred_element_type=f32)
        total = got[: quantities * rows] + got[quantities * rows :]
        for q in range(quantities):
            out_refs[e][q] = total[q * rows : (q + 1) * rows]


def parities(axes):
    return [lax.rem(lax.axis_index(axis), 2) for axis in axes]


def predict_kernel(axes, dofs_in, star_in, stiff_in, lists_in, first_ref, late_ref, s0, s1, s2, s3,
                   w_ref, v_ref, t_ref, stiff_ref, dofs_ref, star_ref, lists_ref, sems):
    h = step_length
    rows = first_ref.shape[1]
    pairs = [(stiff_in, stiff_ref), (dofs_in, dofs_ref), (star_in, star_ref), (lists_in, lists_ref)]
    copies = [pltpu.make_async_copy(src, dst, sems.at[i]) for i, (src, dst) in enumerate(pairs)]
    for copy in copies:
        copy.start()
    copies[0].wait()
    w_ref[...] = series_weights(stiff_ref, rows, False)
    for copy in copies[1:]:
        copy.wait()
    for q in range(dofs_ref.shape[0]):
        v_ref[q] = pad_rows(dofs_ref[q], rows)
    sums = [(first_ref, weights_of(0.0, h)), (late_ref, weights_of(h, 2 * h))]
    series(w_ref, v_ref, t_ref, star_ref, sums)
    pack_sends(first_ref, lists_ref, [s0, s1, s2, s3], parities(axes))


def effective(type_ref, near_ref, face_ref):
    kind = type_ref[...]
    n = kind.shape[1]
    index = jnp.where(kind == 0, near_ref[...], jnp.where(kind == 1, iota(kind.shape, 1), -1))
    source = jnp.where(kind == 0, face_ref[...], jnp.where(kind == 1, iota(kind.shape, 0), 0))
    return index, source


def across_weights(project_ref):
    faces_basis, faces, count = project_ref.shape
    main = (count // 8) * 8
    rest = count - main
    width = faces * count
    col = iota((count, 3 * width), 1) % width
    basis = jnp.where(col < faces * main, col % main, main + (col - faces * main) % rest)
    rep = (basis == iota((count, 3 * width), 0)).astype(bf16)
    tall = faces_basis * faces
    grow = (iota((tall, faces_basis), 0) // faces == iota((tall, faces_basis), 1)).astype(bf16)
    col = iota((tall, 3 * width), 1)
    inner = col % width
    owner = jnp.where(inner < faces * main, inner // main, (inner - faces * main) // rest)
    mine = owner == iota((tall, 3 * width), 0) % faces
    out = []
    for g in range(faces):
        matrix = jnp.concatenate([project_ref[b, g : g + 1] for b in range(faces_basis)], axis=0)
        high, low = spread(matrix, rep, False)
        high = jnp.dot(grow, high.astype(bf16), preferred_element_type=f32)
        low = jnp.dot(grow, low.astype(bf16), preferred_element_type=f32)
        out.append(jnp.where(mine, jnp.where(col < 2 * width, high, low), 0.0))
    return jnp.concatenate(out, axis=0).astype(bf16)


def across_operand(picked, q, rows, height):
    parts = []
    for part in range(2):
        start = part * height + q * rows
        main = [ref[start : start + 16] for ref in picked]
        rest = [ref[start + 16 : start + 24] for ref in picked]
        lower = iota(rest[0].shape, 0) < 4
        parts.append(
            jnp.concatenate(
                main + [jnp.where(lower, rest[0], rest[1]), jnp.where(lower, rest[2], rest[3])], axis=0
            )
        )
    return jnp.concatenate([parts[0], parts[1], parts[0]], axis=0).astype(bf16)


def across_traces(w_ref, picked, source, quantities, rows, store):
    height = quantities * rows
    faces = len(picked)
    tall = w_ref.shape[0] // faces
    wide = jnp.concatenate([source] * (tall // faces), axis=0)
    tests = [wide == g for g in range(faces - 1)]
    for q in range(quantities):
        z = jnp.dot(
            w_ref[...], across_operand(picked, q, rows, height), preferred_element_type=f32
        )
        value = z[(faces - 1) * tall :]
        for g in reversed(range(faces - 1)):
            value = jnp.where(tests[g], z[g * tall : (g + 1) * tall], value)
        store(q, value)


def flux_mix(flux_ref, trace_ref, lane, start):
    quantities, tall = trace_ref.shape[0], trace_ref.shape[1]
    faces = flux_ref.shape[2]
    acc = list(start)
    for q in range(quantities):
        t = trace_ref[q, :, lane]
        for p in range(quantities):
            factor = flux_ref[p, q, :, lane]
            term = jnp.concatenate([factor] * (tall // faces), axis=0) * t
            acc[p] = term if acc[p] is None else acc[p] + term
    return acc


def own_kernel(own_ref, star_ref, minus_in, stiff_ref, project_ref, near_ref, face_ref, type_ref,
               part_ref, g_ref, across_ref, w_ref, wa_ref, trace_ref, t_ref, picked_ref, pick_ref, minus_ref, sem):
    minus_copy = pltpu.make_async_copy(minus_in, minus_ref, sem)
    minus_copy.start()
    quantities, rows, n = own_ref.shape
    faces_basis, faces, count = project_ref.shape
    tall = faces_basis * faces
    flat = jnp.concatenate([project_ref[b] for b in range(faces_basis)], axis=0)
    w_ref[: 9 * rows] = series_weights(stiff_ref, rows, True)
    w_ref[9 * rows :] = jnp.concatenate(block_weights(flat, rows, 3, False), axis=0).astype(bf16)
    wa_ref[...] = across_weights(project_ref)
    for g in range(quantities // 3):
        x = triple(stacked(own_ref, 3 * g, 3))
        t = jnp.dot(w_ref[...], x, preferred_element_type=f32)
        for c in range(3):
            for i in range(3):
                start = (3 * c + i) * rows
                t_ref[c * quantities + 3 * g + i] = t[start : start + rows]
        for i in range(3):
            start = 9 * rows + i * tall
            trace_ref[3 * g + i] = t[start : start + tall]

    index, source = effective(type_ref, near_ref, face_ref)
    high, low = split(stacked(own_ref, 0, quantities))
    both = jnp.concatenate([high, low], axis=0)
    for f in range(faces):
        pick_ref[...] = (iota((n, n), 0) == index[f : f + 1]).astype(bf16)
        picked_ref[f] = jnp.dot(both, pick_ref[...], preferred_element_type=f32)

    def keep(q, value):
        across_ref[q] = value

    across_traces(wa_ref, [picked_ref.at[f] for f in range(faces)], source, quantities, rows, keep)

    minus_copy.wait()

    def tile(lane):
        acc = star_mix(star_ref, t_ref, lane, quantities)
        for p in range(quantities):
            part_ref[p, :, lane] = acc[p]
        acc = flux_mix(minus_ref, trace_ref, lane, [None] * quantities)
        for p in range(quantities):
            g_ref[p, :, lane] = acc[p]

    lane_tiles(n, tile)


def lift_weights(lift_ref, rows):
    faces_basis = lift_ref.shape[0]
    flat = jnp.concatenate([lift_ref[b] for b in range(faces_basis)], axis=0)
    blocks = block_weights(flat, flat.shape[0], 2, True)
    return jnp.concatenate([pad_rows(block, rows) for block in blocks], axis=0).astype(bf16)


def ghost_part(axes, got_refs, plus_ref, project_ref, lift_ref, near_ref, face_ref, type_ref,
               part_ref, g_ref, across_ref, wa_ref, wl_ref, picked_ref, pick_ref, trace_ref, flux_ref, emit):
    quantities, rows, n = part_ref.shape
    faces = project_ref.shape[1]
    count = got_refs[0].shape[2]
    wa_ref[...] = across_weights(project_ref)
    wl_ref[...] = lift_weights(lift_ref, rows)
    index, source = effective(type_ref, near_ref, face_ref)
    parity = parities(axes)
    ghost = index - n
    block = ghost // count
    axis_parity = jnp.where(block < 2, parity[0], parity[1])
    slot = (block // 2) * 2 + jnp.where(block % 2 == 1, axis_parity, 1 - axis_parity)
    column = jnp.where(ghost >= 0, slot * LANES + ghost % count, -1)
    operands = []
    for e in range(DIRS):
        high, low = split(stacked(got_refs[e], 0, quantities))
        both = jnp.concatenate([high, low], axis=0)
        empty = jnp.zeros((both.shape[0], LANES - count), bf16)
        operands.append(jnp.concatenate([both, empty], axis=1))
    operand = jnp.concatenate(operands, axis=1)
    for f in range(faces):
        pick_ref[...] = (iota((DIRS * LANES, n), 0) == column[f : f + 1]).astype(bf16)
        picked_ref[f] = jnp.dot(operand, pick_ref[...], preferred_element_type=f32)

    def keep(q, value):
        trace_ref[q] = across_ref[q] + value

    across_traces(wa_ref, [picked_ref.at[f] for f in range(faces)], source, quantities, rows, keep)

    def tile(lane):
        acc = flux_mix(plus_ref, trace_ref, lane, [g_ref[p, :, lane] for p in range(quantities)])
        for p in range(quantities):
            flux_ref[p, :, lane] = acc[p]

    lane_tiles(n, tile)
    for pair in range(0, quantities, 2):
        two = pair + 1 < quantities
        x = jnp.concatenate(
            [flux_ref[pair], flux_ref[pair + 1] if two else jnp.zeros(flux_ref.shape[1:], f32)], axis=0
        )
        lifted = jnp.dot(wl_ref[...], triple(x), preferred_element_type=f32)
        emit(pair, part_ref[pair] - lifted[:rows])
        if two:
            emit(pair + 1, part_ref[pair + 1] - lifted[rows:])


def middle_kernel(axes, got0, got1, got2, got3, plus_ref, project_ref, lift_ref, near_ref, face_ref, type_ref,
                  part_ref, g_ref, across_ref, dofs_ref, star_ref, stiff_ref, cluster_in, late_ref, lists_ref,
                  midway_ref, second_ref, s0, s1, s2, s3,
                  wa_ref, wl_ref, picked_ref, pick_ref, trace_ref, flux_ref, w_ref, v_ref, t_ref, cluster_ref, sem):
    cluster_copy = pltpu.make_async_copy(cluster_in, cluster_ref, sem)
    cluster_copy.start()
    rows = part_ref.shape[1]
    quantities = part_ref.shape[0]

    def emit(q, change):
        value = pad_rows(dofs_ref[q], rows) + change
        midway_ref[q] = value
        v_ref[q] = value

    ghost_part(axes, [got0, got1, got2, got3], plus_ref, project_ref, lift_ref, near_ref, face_ref, type_ref,
               part_ref, g_ref, across_ref, wa_ref, wl_ref, picked_ref, pick_ref, trace_ref, flux_ref, emit)
    w_ref[...] = series_weights(stiff_ref, rows, False)
    series(w_ref, v_ref, t_ref, star_ref, [(second_ref, weights_of(0.0, step_length))])
    cluster_copy.wait()
    fast = cluster_ref[...][None, :] == 0
    for q in range(quantities):
        second_ref[q] = jnp.where(fast, second_ref[q], late_ref[q])
    pack_sends(second_ref, lists_ref, [s0, s1, s2, s3], parities(axes))


def finish_kernel(axes, got0, got1, got2, got3, plus_ref, project_ref, lift_ref, near_ref, face_ref, type_ref,
                  part_ref, g_ref, across_ref, midway_ref, out_ref,
                  wa_ref, wl_ref, picked_ref, pick_ref, trace_ref, flux_ref):
    count = out_ref.shape[1]

    def emit(q, change):
        out_ref[q] = (midway_ref[q] + change)[:count]

    ghost_part(axes, [got0, got1, got2, got3], plus_ref, project_ref, lift_ref, near_ref, face_ref, type_ref,
               part_ref, g_ref, across_ref, wa_ref, wl_ref, picked_ref, pick_ref, trace_ref, flux_ref, emit)


def call(kernel, name, args, outs, scratch, flops, far=(), vmem_bytes=20 << 20):
    spec = pl.BlockSpec(memory_space=pltpu.VMEM)
    hbm = pl.BlockSpec(memory_space=pltpu.HBM)
    size = sum(4 * math.prod(a.shape) for a in list(args) + list(outs))
    return pl.pallas_call(
        kernel,
        out_shape=[jax.ShapeDtypeStruct(s.shape, s.dtype) for s in outs],
        in_specs=[hbm if i in far else spec for i in range(len(args))],
        out_specs=[spec] * len(outs),
        scratch_shapes=scratch,
        cost_estimate=pl.CostEstimate(flops=flops, bytes_accessed=size, transcendentals=0),
        compiler_params=pltpu.CompilerParams(vmem_limit_bytes=vmem_bytes),
        name=name,
    )(*[pltpu.with_memory_space_constraint(a, pltpu.HBM) if i in far else a for i, a in enumerate(args)])


def exchange(block, axis, offset):
    count = lax.axis_size(axis)
    route = []
    for i in range(offset, count - 1, 2):
        route += [(i, i + 1), (i + 1, i)]
    return lax.ppermute(block, axis, route)


def swap(sends):
    return [
        exchange(sends[0], "px", 0),
        exchange(sends[1], "px", 1),
        exchange(sends[2], "py", 0),
        exchange(sends[3], "py", 1),
    ]


def per_device(dofs, star, flux_minus, flux_plus, stiffness, project, lift, cluster, neighbour, neighbour_face,
               face_type, send_list):
    axes = ("px", "py")
    quantities, count, n = dofs.shape
    faces, faces_basis = project.shape[:2]
    rows = 8 * pl.cdiv(count, 8)
    tall = faces * faces_basis
    width = send_list.shape[1]
    star = jnp.transpose(star, (1, 2, 0, 3))
    minus = jnp.transpose(flux_minus, (1, 2, 0, 3))
    plus = jnp.transpose(flux_plus, (1, 2, 0, 3))
    project = jnp.transpose(project, (1, 0, 2))
    lift = jnp.transpose(lift, (2, 0, 1))

    field = jax.ShapeDtypeStruct((quantities, rows, n), f32)
    traces = jax.ShapeDtypeStruct((quantities, tall, n), f32)
    sends = (jax.ShapeDtypeStruct((quantities, rows, width), f32),) * DIRS
    series_w = pltpu.VMEM((9 * rows, 9 * rows), bf16)
    v_field = pltpu.VMEM((quantities, rows, n), f32)
    t_field = pltpu.VMEM((3 * quantities, rows, n), f32)
    t_trace = pltpu.VMEM((quantities, tall, n), f32)
    across_w = pltpu.VMEM((faces * tall, 3 * faces * count), bf16)
    lift_w = pltpu.VMEM((2 * rows, 6 * tall), bf16)
    picked = pltpu.VMEM((faces, 2 * quantities * rows, n), f32)

    first, late, *out = call(
        functools.partial(predict_kernel, axes), "predict", (dofs, star, stiffness, send_list),
        (field, field, *sends),
        [series_w, v_field, t_field] + [pltpu.VMEM(a.shape, a.dtype) for a in (stiffness, dofs, star, send_list)]
        + [pltpu.SemaphoreType.DMA((4,))], 10_000_000, far=(0, 1, 2, 3))

    def own(buffer, name):
        return call(
            own_kernel, name, (buffer, star, minus, stiffness, project, neighbour, neighbour_face, face_type),
            (field, traces, traces),
            [pltpu.VMEM((9 * rows + 3 * tall, 9 * rows), bf16), across_w, t_trace, t_field, picked,
             pltpu.VMEM((n, n), bf16), pltpu.VMEM(minus.shape, f32), pltpu.SemaphoreType.DMA(())],
            10_000_000, far=(2,))

    ghost_scratch = [across_w, lift_w, picked, pltpu.VMEM((DIRS * LANES, n), bf16), t_trace, t_trace]
    got = swap(out)
    part, g, across = own(first, "own_first")
    midway, second, *out = call(
        functools.partial(middle_kernel, axes), "middle",
        (*got, plus, project, lift, neighbour, neighbour_face, face_type, part, g, across, dofs, star, stiffness,
         cluster, late, send_list),
        (field, field, *sends), ghost_scratch + [series_w, v_field, t_field, pltpu.VMEM((n,), jnp.int32), pltpu.SemaphoreType.DMA(())],
        10_000_000, far=(16,))
    got = swap(out)
    part, g, across = own(second, "own_second")
    (result,) = call(
        functools.partial(finish_kernel, axes), "finish",
        (*got, plus, project, lift, neighbour, neighbour_face, face_type, part, g, across, midway),
        (jax.ShapeDtypeStruct((quantities, count, n), f32),), ghost_scratch, 10_000_000)
    return result


def solution(mesh):
    both = ("px", "py")
    in_specs = (
        P(None, None, both),
        P(None, None, None, both),
        P(None, None, None, both),
        P(None, None, None, both),
        P(),
        P(),
        P(),
        P(both),
        P(None, both),
        P(None, both),
        P(None, both),
        P(None, both),
    )
    return jax.shard_map(
        per_device, mesh=mesh, in_specs=in_specs, out_specs=P(None, None, both), check_vma=False
    )
```

```python
import functools
import math

import jax
import jax.numpy as jnp
from jax import lax
from jax.experimental import pallas as pl
from jax.experimental.pallas import tpu as pltpu
from jax.sharding import PartitionSpec as P

f32, bf16 = jnp.float32, jnp.bfloat16
step_length = 0.5
LANES = 128
DIRS = 4


def weights_of(lower, upper):
    return [
        (upper ** (m + 1) - lower ** (m + 1)) / math.factorial(m + 1) for m in range(4)
    ]


def iota(shape, dim):
    return lax.broadcasted_iota(jnp.int32, shape, dim)


def split(x):
    high = x.astype(bf16)
    return high, (x - high.astype(f32)).astype(bf16)


def triple(x):
    high = x.astype(bf16).astype(f32)
    return jnp.concatenate([high, x - high, high], axis=0).astype(bf16)


def pad_rows(x, rows):
    return jnp.concatenate([x, x[2 * x.shape[0] - rows :]], axis=0)


def spread(matrix, rep, transposed):
    dims = (((0,) if transposed else (1,), (0,)), ((), ()))
    high, low = split(matrix)
    return [
        lax.dot_general(part, rep, dims, preferred_element_type=f32)
        for part in (high, low)
    ]


def block_weights(matrix, inner, copies, transposed):
    count = matrix.shape[0] if transposed else matrix.shape[1]
    width = 3 * copies * inner
    rep = (iota((count, width), 1) % inner == iota((count, width), 0)).astype(bf16)
    high, low = spread(matrix, rep, transposed)
    col = iota(high.shape, 1)
    both = jnp.where(col < 2 * copies * inner, high, low)
    owner = (col % (copies * inner)) // inner
    return [jnp.where(owner == q, both, 0.0) for q in range(copies)]


def series_weights(stiff_ref, rows, transposed):
    out = []
    for c in range(3):
        for block in block_weights(stiff_ref[c], rows, 3, transposed):
            out.append(pad_rows(block, rows))
    return jnp.concatenate(out, axis=0).astype(bf16)


def stacked(ref, first, count):
    return jnp.concatenate([ref[first + i] for i in range(count)], axis=0)


def star_mix(star_ref, t_ref, lane, quantities):
    rows = t_ref.shape[1]
    acc = [None] * quantities
    for c in range(3):
        for q in range(quantities):
            t = t_ref[c * quantities + q, :, lane]
            for p in range(quantities):
                term = jnp.broadcast_to(star_ref[p, q, c : c + 1, lane], (rows, LANES)) * t
                acc[p] = term if acc[p] is None else acc[p] + term
    return acc


def lane_tiles(n, body):
    def one(tile, carry):
        body(pl.ds(pl.multiple_of(tile * LANES, LANES), LANES))
        return carry

    lax.fori_loop(0, n // LANES, one, 0)


def stiff_products(w_ref, v_ref, t_ref, lane):
    quantities, rows = v_ref.shape[:2]
    for g in range(quantities // 3):
        x = jnp.concatenate([v_ref[3 * g + i, :, lane] for i in range(3)], axis=0)
        t = jnp.dot(w_ref[...], triple(x), preferred_element_type=f32)
        for c in range(3):
            for i in range(3):
                start = (3 * c + i) * rows
                t_ref[c * quantities + 3 * g + i, :, lane] = t[start : start + rows]


def series(w_ref, v_ref, t_ref, star_ref, sums, ready=lambda: None):
    quantities, _, n = v_ref.shape
    tiles = n // LANES
    for ref, weights in sums:
        for q in range(quantities):
            ref[q] = weights[0] * v_ref[q]
    stiff_products(w_ref, v_ref, t_ref, pl.ds(0, n))
    ready()
    for m in range(1, 4):

        def tile(index, carry, m=m):
            lane = pl.ds(pl.multiple_of(index * LANES, LANES), LANES)
            acc = star_mix(star_ref, t_ref, lane, quantities)
            for p in range(quantities):
                value = -acc[p]
                if m < 3:
                    v_ref[p, :, lane] = value
                for ref, weights in sums:
                    ref[p, :, lane] += weights[m] * value
            return carry

        lax.fori_loop(0, tiles, tile, 0)
        if m < 3:
            stiff_products(w_ref, v_ref, t_ref, pl.ds(0, n))


def pack_sends(buffer_ref, lists_ref, out_refs, parity):
    quantities, rows, n = buffer_ref.shape
    high, low = split(stacked(buffer_ref, 0, quantities))
    both = jnp.concatenate([high, low], axis=0)
    count = lists_ref.shape[1]
    wanted = lists_ref[...]
    picks = []
    for e in range(DIRS):
        axis = e // 2
        even, odd = (1, 0) if e % 2 == 0 else (0, 1)
        row = jnp.where(
            parity[axis] == 0,
            wanted[2 * axis + even : 2 * axis + even + 1],
            wanted[2 * axis + odd : 2 * axis + odd + 1],
        )
        row = jnp.concatenate([row, jnp.full((1, LANES - count), -1, jnp.int32)], axis=1)
        picks.append((iota((n, LANES), 0) == row).astype(bf16))
    got = jnp.dot(both, jnp.concatenate(picks, axis=1), preferred_element_type=f32)
    total = got[: quantities * rows] + got[quantities * rows :]
    for e in range(DIRS):
        for q in range(quantities):
            out_refs[e][q] = total[q * rows : (q + 1) * rows, e * LANES : e * LANES + count]


def parities(axes):
    return [lax.rem(lax.axis_index(axis), 2) for axis in axes]


def predict_kernel(axes, stiff_in, project_in, lift_in, dofs_in, star_in, lists_in,
                   first_ref, late_ref, s0, s1, s2, s3, w_ref, wo_ref, wa_ref, wl_ref,
                   v_ref, t_ref, stiff_ref, project_ref, lift_ref, dofs_ref, star_ref, lists_ref, sems):
    h = step_length
    rows = first_ref.shape[1]
    pairs = [(stiff_in, stiff_ref), (project_in, project_ref), (lift_in, lift_ref),
             (dofs_in, dofs_ref), (star_in, star_ref), (lists_in, lists_ref)]
    copies = [pltpu.make_async_copy(src, dst, sems.at[i]) for i, (src, dst) in enumerate(pairs)]
    for copy in copies:
        copy.start()
    for copy in copies[:3]:
        copy.wait()
    faces_basis = project_ref.shape[0]
    flat = jnp.concatenate([project_ref[b] for b in range(faces_basis)], axis=0)
    w_ref[...] = series_weights(stiff_ref, rows, False)
    wo_ref[: 9 * rows] = series_weights(stiff_ref, rows, True)
    wo_ref[9 * rows :] = jnp.concatenate(block_weights(flat, rows, 3, False), axis=0).astype(bf16)
    wa_ref[...] = across_weights(project_ref)
    wl_ref[...] = lift_weights(lift_ref, rows)
    copies[3].wait()
    for q in range(dofs_ref.shape[0]):
        v_ref[q] = pad_rows(dofs_ref[q], rows)
    sums = [(first_ref, weights_of(0.0, h)), (late_ref, weights_of(h, 2 * h))]
    series(w_ref, v_ref, t_ref, star_ref, sums, copies[4].wait)
    copies[5].wait()
    pack_sends(first_ref, lists_ref, [s0, s1, s2, s3], parities(axes))


def effective(type_ref, near_ref, face_ref):
    kind = type_ref[...]
    n = kind.shape[1]
    index = jnp.where(kind == 0, near_ref[...], jnp.where(kind == 1, iota(kind.shape, 1), -1))
    source = jnp.where(kind == 0, face_ref[...], jnp.where(kind == 1, iota(kind.shape, 0), 0))
    return index, source


def across_weights(project_ref):
    faces_basis, faces, count = project_ref.shape
    main = (count // 8) * 8
    rest = count - main
    width = faces * count
    col = iota((count, 3 * width), 1) % width
    basis = jnp.where(col < faces * main, col % main, main + (col - faces * main) % rest)
    rep = (basis == iota((count, 3 * width), 0)).astype(bf16)
    tall = faces_basis * faces
    grow = (iota((tall, faces_basis), 0) // faces == iota((tall, faces_basis), 1)).astype(bf16)
    col = iota((tall, 3 * width), 1)
    inner = col % width
    owner = jnp.where(inner < faces * main, inner // main, (inner - faces * main) // rest)
    mine = owner == iota((tall, 3 * width), 0) % faces
    out = []
    for g in range(faces):
        matrix = jnp.concatenate([project_ref[b, g : g + 1] for b in range(faces_basis)], axis=0)
        high, low = spread(matrix, rep, False)
        high = jnp.dot(grow, high.astype(bf16), preferred_element_type=f32)
        low = jnp.dot(grow, low.astype(bf16), preferred_element_type=f32)
        out.append(jnp.where(mine, jnp.where(col < 2 * width, high, low), 0.0))
    return jnp.concatenate(out, axis=0).astype(bf16)


def across_operand(picked, q, rows, height):
    parts = []
    for part in range(2):
        start = part * height + q * rows
        main = [ref[start : start + 16] for ref in picked]
        rest = [ref[start + 16 : start + 24] for ref in picked]
        lower = iota(rest[0].shape, 0) < 4
        parts.append(
            jnp.concatenate(
                main + [jnp.where(lower, rest[0], rest[1]), jnp.where(lower, rest[2], rest[3])], axis=0
            )
        )
    return jnp.concatenate([parts[0], parts[1], parts[0]], axis=0).astype(bf16)


def across_traces(w_ref, picked, source, quantities, rows, store):
    height = quantities * rows
    faces = len(picked)
    tall = w_ref.shape[0] // faces
    wide = jnp.concatenate([source] * (tall // faces), axis=0)
    tests = [wide == g for g in range(faces - 1)]
    n = source.shape[1]
    for first in range(0, quantities, 2):
        group = range(first, min(first + 2, quantities))
        x = jnp.concatenate([across_operand(picked, q, rows, height) for q in group], axis=1)
        z = jnp.dot(w_ref[...], x, preferred_element_type=f32)
        for i, q in enumerate(group):
            mine = z[:, i * n : (i + 1) * n]
            value = mine[(faces - 1) * tall :]
            for g in reversed(range(faces - 1)):
                value = jnp.where(tests[g], mine[g * tall : (g + 1) * tall], value)
            store(q, value)


def flux_mix(flux_ref, trace_ref, lane, start):
    quantities, tall = trace_ref.shape[0], trace_ref.shape[1]
    faces = flux_ref.shape[2]
    acc = list(start)
    for q in range(quantities):
        t = trace_ref[q, :, lane]
        for p in range(quantities):
            factor = flux_ref[p, q, :, lane]
            term = jnp.concatenate([factor] * (tall // faces), axis=0) * t
            acc[p] = term if acc[p] is None else acc[p] + term
    return acc


def gather(operand, index, picked_ref):
    faces, n = index.shape
    picks = [(iota((operand.shape[1], n), 0) == index[f : f + 1]).astype(bf16) for f in range(faces)]
    picked_ref[...] = jnp.dot(operand, jnp.concatenate(picks, axis=1), preferred_element_type=f32)
    return [picked_ref.at[:, f * n : (f + 1) * n] for f in range(faces)]


def own_kernel(own_ref, star_ref, minus_in, w_ref, wa_ref, near_ref, face_ref, type_ref,
               part_ref, g_ref, across_ref, trace_ref, t_ref, picked_ref, minus_ref, sem):
    minus_copy = pltpu.make_async_copy(minus_in, minus_ref, sem)
    minus_copy.start()
    quantities, rows, n = own_ref.shape
    tall = trace_ref.shape[1]
    groups = quantities // 3
    x = jnp.concatenate([triple(stacked(own_ref, 3 * g, 3)) for g in range(groups)], axis=1)
    t = jnp.dot(w_ref[...], x, preferred_element_type=f32)
    for g in range(groups):
        for c in range(3):
            for i in range(3):
                start = (3 * c + i) * rows
                t_ref[c * quantities + 3 * g + i] = t[start : start + rows, g * n : (g + 1) * n]
        for i in range(3):
            start = 9 * rows + i * tall
            trace_ref[3 * g + i] = t[start : start + tall, g * n : (g + 1) * n]

    index, source = effective(type_ref, near_ref, face_ref)
    high, low = split(stacked(own_ref, 0, quantities))
    picked = gather(jnp.concatenate([high, low], axis=0), index, picked_ref)

    def keep(q, value):
        across_ref[q] = value

    across_traces(wa_ref, picked, source, quantities, rows, keep)

    minus_copy.wait()

    def tile(lane):
        acc = star_mix(star_ref, t_ref, lane, quantities)
        for p in range(quantities):
            part_ref[p, :, lane] = acc[p]
        acc = flux_mix(minus_ref, trace_ref, lane, [None] * quantities)
        for p in range(quantities):
            g_ref[p, :, lane] = acc[p]

    lane_tiles(n, tile)


def lift_weights(lift_ref, rows):
    faces_basis = lift_ref.shape[0]
    flat = jnp.concatenate([lift_ref[b] for b in range(faces_basis)], axis=0)
    blocks = block_weights(flat, flat.shape[0], 2, True)
    return jnp.concatenate([pad_rows(block, rows) for block in blocks], axis=0).astype(bf16)


def ghost_part(axes, got_refs, plus_ref, wa_ref, wl_ref, near_ref, face_ref, type_ref,
               part_ref, g_ref, across_ref, picked_ref, trace_ref, flux_ref, emit):
    quantities, rows, n = part_ref.shape
    count = got_refs[0].shape[2]
    index, source = effective(type_ref, near_ref, face_ref)
    parity = parities(axes)
    ghost = index - n
    block = ghost // count
    axis_parity = jnp.where(block < 2, parity[0], parity[1])
    slot = (block // 2) * 2 + jnp.where(block % 2 == 1, axis_parity, 1 - axis_parity)
    column = jnp.where(ghost >= 0, slot * LANES + ghost % count, -1)
    operands = []
    for e in range(DIRS):
        high, low = split(stacked(got_refs[e], 0, quantities))
        both = jnp.concatenate([high, low], axis=0)
        empty = jnp.zeros((both.shape[0], LANES - count), bf16)
        operands.append(jnp.concatenate([both, empty], axis=1))
    picked = gather(jnp.concatenate(operands, axis=1), column, picked_ref)

    def keep(q, value):
        trace_ref[q] = across_ref[q] + value

    across_traces(wa_ref, picked, source, quantities, rows, keep)

    def tile(lane):
        acc = flux_mix(plus_ref, trace_ref, lane, [g_ref[p, :, lane] for p in range(quantities)])
        for p in range(quantities):
            flux_ref[p, :, lane] = acc[p]

    lane_tiles(n, tile)
    pairs = range(0, quantities, 2)
    operands = []
    for pair in pairs:
        other = flux_ref[pair + 1] if pair + 1 < quantities else jnp.zeros(flux_ref.shape[1:], f32)
        operands.append(triple(jnp.concatenate([flux_ref[pair], other], axis=0)))
    lifted = jnp.dot(wl_ref[...], jnp.concatenate(operands, axis=1), preferred_element_type=f32)
    for q in range(quantities):
        row, column = (q % 2) * rows, (q // 2) * n
        emit(q, part_ref[q] - lifted[row : row + rows, column : column + n])


def middle_kernel(axes, got0, got1, got2, got3, plus_ref, wa_ref, wl_ref, near_ref, face_ref, type_ref,
                  part_ref, g_ref, across_ref, dofs_ref, star_ref, w_ref, cluster_in, late_ref, lists_in,
                  midway_ref, second_ref, s0, s1, s2, s3,
                  picked_ref, trace_ref, flux_ref, v_ref, t_ref, cluster_ref, lists_ref, sems):
    copies = [pltpu.make_async_copy(cluster_in, cluster_ref, sems.at[0]),
              pltpu.make_async_copy(lists_in, lists_ref, sems.at[1])]
    for copy in copies:
        copy.start()
    rows = part_ref.shape[1]
    quantities = part_ref.shape[0]

    def emit(q, change):
        value = pad_rows(dofs_ref[q], rows) + change
        midway_ref[q] = value
        v_ref[q] = value

    ghost_part(axes, [got0, got1, got2, got3], plus_ref, wa_ref, wl_ref, near_ref, face_ref, type_ref,
               part_ref, g_ref, across_ref, picked_ref, trace_ref, flux_ref, emit)
    series(w_ref, v_ref, t_ref, star_ref, [(second_ref, weights_of(0.0, step_length))])
    for copy in copies:
        copy.wait()
    fast = cluster_ref[...][None, :] == 0
    for q in range(quantities):
        second_ref[q] = jnp.where(fast, second_ref[q], late_ref[q])
    pack_sends(second_ref, lists_ref, [s0, s1, s2, s3], parities(axes))


def finish_kernel(axes, got0, got1, got2, got3, plus_ref, wa_ref, wl_ref, near_ref, face_ref, type_ref,
                  part_ref, g_ref, across_ref, midway_ref, out_ref, picked_ref, trace_ref, flux_ref):
    count = out_ref.shape[1]

    def emit(q, change):
        out_ref[q] = (midway_ref[q] + change)[:count]

    ghost_part(axes, [got0, got1, got2, got3], plus_ref, wa_ref, wl_ref, near_ref, face_ref, type_ref,
               part_ref, g_ref, across_ref, picked_ref, trace_ref, flux_ref, emit)


def call(kernel, name, args, outs, scratch, flops, far=(), vmem_bytes=20 << 20):
    spec = pl.BlockSpec(memory_space=pltpu.VMEM)
    hbm = pl.BlockSpec(memory_space=pltpu.HBM)
    size = sum(4 * math.prod(a.shape) for a in list(args) + list(outs))
    return pl.pallas_call(
        kernel,
        out_shape=[jax.ShapeDtypeStruct(s.shape, s.dtype) for s in outs],
        in_specs=[hbm if i in far else spec for i in range(len(args))],
        out_specs=[spec] * len(outs),
        scratch_shapes=scratch,
        cost_estimate=pl.CostEstimate(flops=flops, bytes_accessed=size, transcendentals=0),
        compiler_params=pltpu.CompilerParams(vmem_limit_bytes=vmem_bytes),
        name=name,
    )(*[pltpu.with_memory_space_constraint(a, pltpu.HBM) if i in far else a for i, a in enumerate(args)])


def exchange(block, axis, offset):
    count = lax.axis_size(axis)
    route = []
    for i in range(offset, count - 1, 2):
        route += [(i, i + 1), (i + 1, i)]
    return lax.ppermute(block, axis, route)


def swap(sends):
    return [
        exchange(sends[0], "px", 0),
        exchange(sends[1], "px", 1),
        exchange(sends[2], "py", 0),
        exchange(sends[3], "py", 1),
    ]


def per_device(dofs, star, flux_minus, flux_plus, stiffness, project, lift, cluster, neighbour, neighbour_face,
               face_type, send_list):
    axes = ("px", "py")
    quantities, count, n = dofs.shape
    faces, faces_basis = project.shape[:2]
    rows = 8 * pl.cdiv(count, 8)
    tall = faces * faces_basis
    width = send_list.shape[1]
    star = jnp.transpose(star, (1, 2, 0, 3))
    minus = jnp.transpose(flux_minus, (1, 2, 0, 3))
    plus = jnp.transpose(flux_plus, (1, 2, 0, 3))
    project = jnp.transpose(project, (1, 0, 2))
    lift = jnp.transpose(lift, (2, 0, 1))

    field = jax.ShapeDtypeStruct((quantities, rows, n), f32)
    traces = jax.ShapeDtypeStruct((quantities, tall, n), f32)
    sends = (jax.ShapeDtypeStruct((quantities, rows, width), f32),) * DIRS
    weights = (
        jax.ShapeDtypeStruct((9 * rows, 9 * rows), bf16),
        jax.ShapeDtypeStruct((9 * rows + 3 * tall, 9 * rows), bf16),
        jax.ShapeDtypeStruct((faces * tall, 3 * faces * count), bf16),
        jax.ShapeDtypeStruct((2 * rows, 6 * tall), bf16),
    )
    v_field = pltpu.VMEM((quantities, rows, n), f32)
    t_field = pltpu.VMEM((3 * quantities, rows, n), f32)
    t_trace = pltpu.VMEM((quantities, tall, n), f32)
    picked = pltpu.VMEM((2 * quantities * rows, faces * n), f32)

    inputs = (stiffness, project, lift, dofs, star, send_list)
    first, late, *out = call(
        functools.partial(predict_kernel, axes), "predict", inputs, (field, field, *sends, *weights),
        [v_field, t_field] + [pltpu.VMEM(a.shape, a.dtype) for a in inputs]
        + [pltpu.SemaphoreType.DMA((len(inputs),))], 10_000_000, far=range(len(inputs)))
    out, (w, wo, wa, wl) = out[:DIRS], out[DIRS:]

    def own(buffer, name):
        return call(
            own_kernel, name, (buffer, star, minus, wo, wa, neighbour, neighbour_face, face_type),
            (field, traces, traces),
            [t_trace, t_field, picked, pltpu.VMEM(minus.shape, f32), pltpu.SemaphoreType.DMA(())],
            10_000_000, far=(2,))

    ghost_scratch = [picked, t_trace, t_trace]
    got = swap(out)
    part, g, across = own(first, "own_first")
    midway, second, *out = call(
        functools.partial(middle_kernel, axes), "middle",
        (*got, plus, wa, wl, neighbour, neighbour_face, face_type, part, g, across, dofs, star, w,
         cluster, late, send_list),
        (field, field, *sends),
        ghost_scratch + [v_field, t_field, pltpu.VMEM((n,), jnp.int32), pltpu.VMEM(send_list.shape, jnp.int32),
                         pltpu.SemaphoreType.DMA((2,))],
        10_000_000, far=(16, 18))
    got = swap(out)
    part, g, across = own(second, "own_second")
    (result,) = call(
        functools.partial(finish_kernel, axes), "finish",
        (*got, plus, wa, wl, neighbour, neighbour_face, face_type, part, g, across, midway),
        (jax.ShapeDtypeStruct((quantities, count, n), f32),), ghost_scratch, 10_000_000)
    return result


def solution(mesh):
    both = ("px", "py")
    in_specs = (
        P(None, None, both),
        P(None, None, None, both),
        P(None, None, None, both),
        P(None, None, None, both),
        P(),
        P(),
        P(),
        P(both),
        P(None, both),
        P(None, both),
        P(None, both),
        P(None, both),
    )
    return jax.shard_map(
        per_device, mesh=mesh, in_specs=in_specs, out_specs=P(None, None, both), check_vma=False
    )
```

```python
import functools
import math

import jax
import jax.numpy as jnp
from jax import lax
from jax.experimental import pallas as pl
from jax.experimental.pallas import tpu as pltpu
from jax.sharding import PartitionSpec as P

f32, bf16 = jnp.float32, jnp.bfloat16
step_length = 0.5
LANES = 128
DIRS = 4


def weights_of(lower, upper):
    return [
        (upper ** (m + 1) - lower ** (m + 1)) / math.factorial(m + 1) for m in range(4)
    ]


def iota(shape, dim):
    return lax.broadcasted_iota(jnp.int32, shape, dim)


def split(x):
    high = x.astype(bf16)
    return high, (x - high.astype(f32)).astype(bf16)


def triple(x):
    high = x.astype(bf16).astype(f32)
    return jnp.concatenate([high, x - high, high], axis=0).astype(bf16)


def pad_rows(x, rows):
    return jnp.concatenate([x, x[2 * x.shape[0] - rows :]], axis=0)


def spread(matrix, rep, transposed):
    dims = (((0,) if transposed else (1,), (0,)), ((), ()))
    high, low = split(matrix)
    return [
        lax.dot_general(part, rep, dims, preferred_element_type=f32)
        for part in (high, low)
    ]


def block_weights(matrix, inner, copies, transposed):
    count = matrix.shape[0] if transposed else matrix.shape[1]
    width = 3 * copies * inner
    rep = (iota((count, width), 1) % inner == iota((count, width), 0)).astype(bf16)
    high, low = spread(matrix, rep, transposed)
    col = iota(high.shape, 1)
    both = jnp.where(col < 2 * copies * inner, high, low)
    owner = (col % (copies * inner)) // inner
    return [jnp.where(owner == q, both, 0.0) for q in range(copies)]


def series_weights(stiff_ref, rows, transposed):
    out = []
    for c in range(3):
        for block in block_weights(stiff_ref[c], rows, 3, transposed):
            out.append(pad_rows(block, rows))
    return jnp.concatenate(out, axis=0).astype(bf16)


def stacked(ref, first, count):
    return jnp.concatenate([ref[first + i] for i in range(count)], axis=0)


def star_mix(star_ref, t_ref, lane, quantities):
    rows = t_ref.shape[1]
    within = lane if t_ref.shape[2] > LANES else pl.ds(0, LANES)
    acc = [None] * quantities
    for c in range(3):
        for q in range(quantities):
            t = t_ref[c * quantities + q, :, within]
            for p in range(quantities):
                term = jnp.broadcast_to(star_ref[p, q, c : c + 1, lane], (rows, LANES)) * t
                acc[p] = term if acc[p] is None else acc[p] + term
    return acc


def lane_tiles(n, body):
    def one(tile, carry):
        body(pl.ds(pl.multiple_of(tile * LANES, LANES), LANES))
        return carry

    lax.fori_loop(0, n // LANES, one, 0)


def stiff_products(w_ref, v_ref, t_ref):
    quantities, rows = v_ref.shape[:2]
    for g in range(quantities // 3):
        t = jnp.dot(w_ref[...], triple(stacked(v_ref, 3 * g, 3)), preferred_element_type=f32)
        for c in range(3):
            for i in range(3):
                start = (3 * c + i) * rows
                t_ref[c * quantities + 3 * g + i] = t[start : start + rows]


def series(w_ref, v_refs, t_refs, star_ref, sums, ready=lambda: None):
    quantities = v_refs[0].shape[0]
    lanes = [pl.ds(i * LANES, LANES) for i in range(len(v_refs))]
    for v_ref, t_ref, lane in zip(v_refs, t_refs, lanes):
        for ref, weights in sums:
            for q in range(quantities):
                ref[q, :, lane] = weights[0] * v_ref[q]
        stiff_products(w_ref, v_ref, t_ref)
    ready()

    def step(degree, last):
        def weight(weights):
            if last:
                return weights[3]
            return jnp.where(degree == 0, weights[1], weights[2])

        for v_ref, t_ref, lane in zip(v_refs, t_refs, lanes):
            acc = star_mix(star_ref, t_ref, lane, quantities)
            for p in range(quantities):
                value = -acc[p]
                if not last:
                    v_ref[p] = value
                for ref, weights in sums:
                    ref[p, :, lane] += weight(weights) * value
            if not last:
                stiff_products(w_ref, v_ref, t_ref)

    def body(degree, carry):
        step(degree, False)
        return carry

    lax.fori_loop(0, 2, body, 0)
    step(2, True)


def pack_sends(buffer_ref, lists_ref, out_refs, parity):
    quantities, rows, n = buffer_ref.shape
    high, low = split(stacked(buffer_ref, 0, quantities))
    both = jnp.concatenate([high, low], axis=0)
    count = lists_ref.shape[1]
    wanted = lists_ref[...]
    picks = []
    for e in range(DIRS):
        axis = e // 2
        even, odd = (1, 0) if e % 2 == 0 else (0, 1)
        row = jnp.where(
            parity[axis] == 0,
            wanted[2 * axis + even : 2 * axis + even + 1],
            wanted[2 * axis + odd : 2 * axis + odd + 1],
        )
        row = jnp.concatenate([row, jnp.full((1, LANES - count), -1, jnp.int32)], axis=1)
        picks.append((iota((n, LANES), 0) == row).astype(bf16))
    got = jnp.dot(both, jnp.concatenate(picks, axis=1), preferred_element_type=f32)
    total = got[: quantities * rows] + got[quantities * rows :]
    for e in range(DIRS):
        for q in range(quantities):
            out_refs[e][q] = total[q * rows : (q + 1) * rows, e * LANES : e * LANES + count]


def parities(axes):
    return [lax.rem(lax.axis_index(axis), 2) for axis in axes]


def predict_kernel(axes, *refs):
    sources, (stiff_ref, project_ref, lift_ref, sems), refs = refs[:12], refs[31:35], refs[12:31] + refs[35:]
    first_ref, late_ref, s0, s1, s2, s3, w_ref, wo_ref, wa_ref, wl_ref = refs[:10]
    kept, tiles = refs[10:19], refs[19:]
    dofs_ref, star_ref, lists_ref = kept[:3]
    v_refs, t_refs = tiles[::2], tiles[1::2]
    h = step_length
    rows = first_ref.shape[1]
    targets = (stiff_ref, project_ref, lift_ref) + tuple(kept)
    copies = [pltpu.make_async_copy(src, dst, sems.at[i]) for i, (src, dst) in enumerate(zip(sources, targets))]
    for copy in copies:
        copy.start()
    for copy in copies[:3]:
        copy.wait()
    faces_basis = project_ref.shape[0]
    flat = jnp.concatenate([project_ref[b] for b in range(faces_basis)], axis=0)
    w_ref[...] = series_weights(stiff_ref, rows, False)
    wo_ref[: 9 * rows] = series_weights(stiff_ref, rows, True)
    wo_ref[9 * rows :] = jnp.concatenate(block_weights(flat, rows, 3, False), axis=0).astype(bf16)
    wa_ref[...] = across_weights(project_ref)
    wl_ref[...] = lift_weights(lift_ref, rows)
    copies[3].wait()
    for q in range(dofs_ref.shape[0]):
        for i, v_ref in enumerate(v_refs):
            v_ref[q] = pad_rows(dofs_ref[q, :, i * LANES : (i + 1) * LANES], rows)
    sums = [(first_ref, weights_of(0.0, h)), (late_ref, weights_of(h, 2 * h))]
    series(w_ref, v_refs, t_refs, star_ref, sums, copies[4].wait)
    for copy in copies[5:]:
        copy.wait()
    pack_sends(first_ref, lists_ref, [s0, s1, s2, s3], parities(axes))


def effective(type_ref, near_ref, face_ref):
    kind = type_ref[...]
    n = kind.shape[1]
    index = jnp.where(kind == 0, near_ref[...], jnp.where(kind == 1, iota(kind.shape, 1), -1))
    source = jnp.where(kind == 0, face_ref[...], jnp.where(kind == 1, iota(kind.shape, 0), 0))
    return index, source


def across_weights(project_ref):
    faces_basis, faces, count = project_ref.shape
    main = (count // 8) * 8
    rest = count - main
    width = faces * count
    col = iota((count, 3 * width), 1) % width
    basis = jnp.where(col < faces * main, col % main, main + (col - faces * main) % rest)
    rep = (basis == iota((count, 3 * width), 0)).astype(bf16)
    tall = faces_basis * faces
    grow = (iota((tall, faces_basis), 0) // faces == iota((tall, faces_basis), 1)).astype(bf16)
    col = iota((tall, 3 * width), 1)
    inner = col % width
    owner = jnp.where(inner < faces * main, inner // main, (inner - faces * main) // rest)
    mine = owner == iota((tall, 3 * width), 0) % faces
    out = []
    for g in range(faces):
        matrix = jnp.concatenate([project_ref[b, g : g + 1] for b in range(faces_basis)], axis=0)
        high, low = spread(matrix, rep, False)
        high = jnp.dot(grow, high.astype(bf16), preferred_element_type=f32)
        low = jnp.dot(grow, low.astype(bf16), preferred_element_type=f32)
        out.append(jnp.where(mine, jnp.where(col < 2 * width, high, low), 0.0))
    return jnp.concatenate(out, axis=0).astype(bf16)


def across_operand(picked, q, rows, height):
    parts = []
    for part in range(2):
        start = part * height + q * rows
        main = [ref[start : start + 16] for ref in picked]
        rest = [ref[start + 16 : start + 24] for ref in picked]
        lower = iota(rest[0].shape, 0) < 4
        parts.append(
            jnp.concatenate(
                main + [jnp.where(lower, rest[0], rest[1]), jnp.where(lower, rest[2], rest[3])], axis=0
            )
        )
    return jnp.concatenate([parts[0], parts[1], parts[0]], axis=0).astype(bf16)


def across_traces(w_ref, picked, source, quantities, rows, store):
    height = quantities * rows
    faces = len(picked)
    tall = w_ref.shape[0] // faces
    wide = jnp.concatenate([source] * (tall // faces), axis=0)
    tests = [wide == g for g in range(faces - 1)]
    n = source.shape[1]
    for first in range(0, quantities, 2):
        group = range(first, min(first + 2, quantities))
        x = jnp.concatenate([across_operand(picked, q, rows, height) for q in group], axis=1)
        z = jnp.dot(w_ref[...], x, preferred_element_type=f32)
        for i, q in enumerate(group):
            mine = z[:, i * n : (i + 1) * n]
            value = mine[(faces - 1) * tall :]
            for g in reversed(range(faces - 1)):
                value = jnp.where(tests[g], mine[g * tall : (g + 1) * tall], value)
            store(q, value)


def flux_mix(flux_ref, trace_ref, lane, start):
    quantities, tall = trace_ref.shape[0], trace_ref.shape[1]
    faces = flux_ref.shape[2]
    acc = list(start)
    for q in range(quantities):
        t = trace_ref[q, :, lane]
        for p in range(quantities):
            factor = flux_ref[p, q, :, lane]
            term = jnp.concatenate([factor] * (tall // faces), axis=0) * t
            acc[p] = term if acc[p] is None else acc[p] + term
    return acc


def gather(operand, index, picked_ref, other_ref=None):
    faces, n = index.shape
    picks = [(iota((operand.shape[1], n), 0) == index[f : f + 1]).astype(bf16) for f in range(faces)]
    got = jnp.dot(operand, jnp.concatenate(picks, axis=1), preferred_element_type=f32)
    picked_ref[...] = got if other_ref is None else got + other_ref[...]
    return [picked_ref.at[:, f * n : (f + 1) * n] for f in range(faces)]


def own_kernel(own_ref, star_ref, minus_ref, w_ref, near_ref, face_ref, type_ref,
               part_ref, g_ref, picked_ref, trace_ref, t_ref):
    quantities, rows, n = own_ref.shape
    tall = trace_ref.shape[1]
    groups = quantities // 3
    x = jnp.concatenate([triple(stacked(own_ref, 3 * g, 3)) for g in range(groups)], axis=1)
    t = jnp.dot(w_ref[...], x, preferred_element_type=f32)
    for g in range(groups):
        for c in range(3):
            for i in range(3):
                start = (3 * c + i) * rows
                t_ref[c * quantities + 3 * g + i] = t[start : start + rows, g * n : (g + 1) * n]
        for i in range(3):
            start = 9 * rows + i * tall
            trace_ref[3 * g + i] = t[start : start + tall, g * n : (g + 1) * n]

    index, _ = effective(type_ref, near_ref, face_ref)
    high, low = split(stacked(own_ref, 0, quantities))
    gather(jnp.concatenate([high, low], axis=0), index, picked_ref)

    def tile(lane):
        acc = star_mix(star_ref, t_ref, lane, quantities)
        for p in range(quantities):
            part_ref[p, :, lane] = acc[p]
        acc = flux_mix(minus_ref, trace_ref, lane, [None] * quantities)
        for p in range(quantities):
            g_ref[p, :, lane] = acc[p]

    lane_tiles(n, tile)


def lift_weights(lift_ref, rows):
    faces_basis = lift_ref.shape[0]
    flat = jnp.concatenate([lift_ref[b] for b in range(faces_basis)], axis=0)
    blocks = block_weights(flat, flat.shape[0], 2, True)
    return jnp.concatenate([pad_rows(block, rows) for block in blocks], axis=0).astype(bf16)


def ghost_part(axes, got_refs, plus_ref, wa_ref, wl_ref, near_ref, face_ref, type_ref,
               part_ref, g_ref, own_picked_ref, picked_ref, trace_ref, flux_ref, emit):
    quantities, rows, n = part_ref.shape
    count = got_refs[0].shape[2]
    index, source = effective(type_ref, near_ref, face_ref)
    parity = parities(axes)
    ghost = index - n
    block = ghost // count
    axis_parity = jnp.where(block < 2, parity[0], parity[1])
    slot = (block // 2) * 2 + jnp.where(block % 2 == 1, axis_parity, 1 - axis_parity)
    column = jnp.where(ghost >= 0, slot * LANES + ghost % count, -1)
    operands = []
    for e in range(DIRS):
        high, low = split(stacked(got_refs[e], 0, quantities))
        both = jnp.concatenate([high, low], axis=0)
        empty = jnp.zeros((both.shape[0], LANES - count), bf16)
        operands.append(jnp.concatenate([both, empty], axis=1))
    picked = gather(jnp.concatenate(operands, axis=1), column, picked_ref, own_picked_ref)

    def keep(q, value):
        trace_ref[q] = value

    across_traces(wa_ref, picked, source, quantities, rows, keep)

    def tile(lane):
        acc = flux_mix(plus_ref, trace_ref, lane, [g_ref[p, :, lane] for p in range(quantities)])
        for p in range(quantities):
            flux_ref[p, :, lane] = acc[p]

    lane_tiles(n, tile)
    pairs = range(0, quantities, 2)
    operands = []
    for pair in pairs:
        other = flux_ref[pair + 1] if pair + 1 < quantities else jnp.zeros(flux_ref.shape[1:], f32)
        operands.append(triple(jnp.concatenate([flux_ref[pair], other], axis=0)))
    lifted = jnp.dot(wl_ref[...], jnp.concatenate(operands, axis=1), preferred_element_type=f32)
    for q in range(quantities):
        row, column = (q % 2) * rows, (q // 2) * n
        emit(q, part_ref[q] - lifted[row : row + rows, column : column + n])


def middle_kernel(axes, got0, got1, got2, got3, plus_ref, wa_ref, wl_ref, near_ref, face_ref, type_ref,
                  part_ref, g_ref, own_picked_ref, dofs_ref, star_ref, w_ref, cluster_ref, late_ref, lists_ref,
                  midway_ref, second_ref, s0, s1, s2, s3,
                  picked_ref, trace_ref, flux_ref, *tiles):
    v_refs, t_refs = tiles[::2], tiles[1::2]
    rows = part_ref.shape[1]
    quantities = part_ref.shape[0]

    def emit(q, change):
        value = pad_rows(dofs_ref[q], rows) + change
        midway_ref[q] = value
        for i, v_ref in enumerate(v_refs):
            v_ref[q] = value[:, i * LANES : (i + 1) * LANES]

    ghost_part(axes, [got0, got1, got2, got3], plus_ref, wa_ref, wl_ref, near_ref, face_ref, type_ref,
               part_ref, g_ref, own_picked_ref, picked_ref, trace_ref, flux_ref, emit)
    series(w_ref, v_refs, t_refs, star_ref, [(second_ref, weights_of(0.0, step_length))])
    fast = cluster_ref[...][None, :] == 0
    for q in range(quantities):
        second_ref[q] = jnp.where(fast, second_ref[q], late_ref[q])
    pack_sends(second_ref, lists_ref, [s0, s1, s2, s3], parities(axes))


def finish_kernel(axes, got0, got1, got2, got3, plus_ref, wa_ref, wl_ref, near_ref, face_ref, type_ref,
                  part_ref, g_ref, own_picked_ref, midway_ref, out_ref, picked_ref, trace_ref, flux_ref):
    count = out_ref.shape[1]

    def emit(q, change):
        out_ref[q] = (midway_ref[q] + change)[:count]

    ghost_part(axes, [got0, got1, got2, got3], plus_ref, wa_ref, wl_ref, near_ref, face_ref, type_ref,
               part_ref, g_ref, own_picked_ref, picked_ref, trace_ref, flux_ref, emit)


def call(kernel, name, args, outs, scratch, flops, far=(), vmem_bytes=20 << 20):
    spec = pl.BlockSpec(memory_space=pltpu.VMEM)
    hbm = pl.BlockSpec(memory_space=pltpu.HBM)
    size = sum(4 * math.prod(a.shape) for a in list(args) + list(outs))
    return pl.pallas_call(
        kernel,
        out_shape=[jax.ShapeDtypeStruct(s.shape, s.dtype) for s in outs],
        in_specs=[hbm if i in far else spec for i in range(len(args))],
        out_specs=[spec] * len(outs),
        scratch_shapes=scratch,
        cost_estimate=pl.CostEstimate(flops=flops, bytes_accessed=size, transcendentals=0),
        compiler_params=pltpu.CompilerParams(vmem_limit_bytes=vmem_bytes),
        name=name,
    )(*[pltpu.with_memory_space_constraint(a, pltpu.HBM) if i in far else a for i, a in enumerate(args)])


def exchange(block, axis, offset):
    count = lax.axis_size(axis)
    route = []
    for i in range(offset, count - 1, 2):
        route += [(i, i + 1), (i + 1, i)]
    return lax.ppermute(block, axis, route)


def swap(sends):
    return [
        exchange(sends[0], "px", 0),
        exchange(sends[1], "px", 1),
        exchange(sends[2], "py", 0),
        exchange(sends[3], "py", 1),
    ]


def per_device(dofs, star, flux_minus, flux_plus, stiffness, project, lift, cluster, neighbour, neighbour_face,
               face_type, send_list):
    axes = ("px", "py")
    quantities, count, n = dofs.shape
    faces, faces_basis = project.shape[:2]
    rows = 8 * pl.cdiv(count, 8)
    tall = faces * faces_basis
    width = send_list.shape[1]
    star = jnp.transpose(star, (1, 2, 0, 3))
    minus = jnp.transpose(flux_minus, (1, 2, 0, 3))
    plus = jnp.transpose(flux_plus, (1, 2, 0, 3))
    project = jnp.transpose(project, (1, 0, 2))
    lift = jnp.transpose(lift, (2, 0, 1))

    field = jax.ShapeDtypeStruct((quantities, rows, n), f32)
    traces = jax.ShapeDtypeStruct((quantities, tall, n), f32)
    sends = (jax.ShapeDtypeStruct((quantities, rows, width), f32),) * DIRS
    weights = (
        jax.ShapeDtypeStruct((9 * rows, 9 * rows), bf16),
        jax.ShapeDtypeStruct((9 * rows + 3 * tall, 9 * rows), bf16),
        jax.ShapeDtypeStruct((faces * tall, 3 * faces * count), bf16),
        jax.ShapeDtypeStruct((2 * rows, 6 * tall), bf16),
    )
    tiles = [pltpu.VMEM((quantities, rows, LANES), f32), pltpu.VMEM((3 * quantities, rows, LANES), f32)] * (n // LANES)
    t_field = pltpu.VMEM((3 * quantities, rows, n), f32)
    t_trace = pltpu.VMEM((quantities, tall, n), f32)
    picked = pltpu.VMEM((2 * quantities * rows, faces * n), f32)

    local = (stiffness, project, lift)
    kept = (dofs, star, send_list, minus, plus, neighbour, neighbour_face, face_type, cluster)
    inputs = local + kept
    first, late, *out = call(
        functools.partial(predict_kernel, axes), "predict", inputs,
        (field, field, *sends, *weights, *(jax.ShapeDtypeStruct(a.shape, a.dtype) for a in kept)),
        [pltpu.VMEM(a.shape, a.dtype) for a in local] + [pltpu.SemaphoreType.DMA((len(inputs),))] + tiles,
        10_000_000, far=range(len(inputs)))
    out, (w, wo, wa, wl), kept = out[:DIRS], out[DIRS : 2 * DIRS], out[2 * DIRS :]
    dofs, star, send_list, minus, plus, neighbour, neighbour_face, face_type, cluster = kept

    def own(buffer, name):
        return call(
            own_kernel, name, (buffer, star, minus, wo, neighbour, neighbour_face, face_type),
            (field, traces, jax.ShapeDtypeStruct((2 * quantities * rows, faces * n), f32)),
            [t_trace, t_field], 10_000_000)

    ghost_scratch = [picked, t_trace, t_trace]
    got = swap(out)
    part, g, chosen = own(first, "own_first")
    midway, second, *out = call(
        functools.partial(middle_kernel, axes), "middle",
        (*got, plus, wa, wl, neighbour, neighbour_face, face_type, part, g, chosen, dofs, star, w,
         cluster, late, send_list),
        (field, field, *sends),
        ghost_scratch + tiles, 10_000_000)
    got = swap(out)
    part, g, chosen = own(second, "own_second")
    (result,) = call(
        functools.partial(finish_kernel, axes), "finish",
        (*got, plus, wa, wl, neighbour, neighbour_face, face_type, part, g, chosen, midway),
        (jax.ShapeDtypeStruct((quantities, count, n), f32),), ghost_scratch, 10_000_000)
    return result


def solution(mesh):
    both = ("px", "py")
    in_specs = (
        P(None, None, both),
        P(None, None, None, both),
        P(None, None, None, both),
        P(None, None, None, both),
        P(),
        P(),
        P(),
        P(both),
        P(None, both),
        P(None, both),
        P(None, both),
        P(None, both),
    )
    return jax.shard_map(
        per_device, mesh=mesh, in_specs=in_specs, out_specs=P(None, None, both), check_vma=False
    )
```

```python
import functools
import math

import jax
import jax.numpy as jnp
from jax import lax
from jax.experimental import pallas as pl
from jax.experimental.pallas import tpu as pltpu
from jax.sharding import PartitionSpec as P

f32, bf16 = jnp.float32, jnp.bfloat16
step_length = 0.5
LANES = 128
DIRS = 4


def weights_of(lower, upper):
    return [
        (upper ** (m + 1) - lower ** (m + 1)) / math.factorial(m + 1) for m in range(4)
    ]


def iota(shape, dim):
    return lax.broadcasted_iota(jnp.int32, shape, dim)


def split(x):
    high = x.astype(bf16)
    return high, (x - high.astype(f32)).astype(bf16)


def triple(x):
    high = x.astype(bf16).astype(f32)
    return jnp.concatenate([high, x - high, high], axis=0).astype(bf16)


def pad_rows(x, rows):
    return jnp.concatenate([x, x[2 * x.shape[0] - rows :]], axis=0)


def spread(matrix, rep, transposed):
    dims = (((0,) if transposed else (1,), (0,)), ((), ()))
    high, low = split(matrix)
    return [
        lax.dot_general(part, rep, dims, preferred_element_type=f32)
        for part in (high, low)
    ]


def block_weights(matrix, inner, copies, transposed):
    count = matrix.shape[0] if transposed else matrix.shape[1]
    width = 3 * copies * inner
    rep = (iota((count, width), 1) % inner == iota((count, width), 0)).astype(bf16)
    high, low = spread(matrix, rep, transposed)
    col = iota(high.shape, 1)
    both = jnp.where(col < 2 * copies * inner, high, low)
    owner = (col % (copies * inner)) // inner
    return [jnp.where(owner == q, both, 0.0) for q in range(copies)]


MAIN = 16


def rest_pairs():
    return [(k, k + 1 if k + 1 < 9 else None) for k in range(0, 9, 2)]


def series_weights(stiff_ref, rows, transposed):
    blocks = []
    for c in range(3):
        blocks += block_weights(stiff_ref[c], rows, 3, transposed)
    out = [block[:MAIN] for block in blocks]
    for one, other in rest_pairs():
        tail = blocks[one][MAIN:]
        out += [tail, jnp.zeros_like(tail) if other is None else blocks[other][MAIN:]]
    return jnp.concatenate(out, axis=0).astype(bf16)


def rest_factors(star_ref, out_ref):
    quantities, _, _, n = star_ref.shape
    lower = iota((8, n), 0) < 4
    for p in range(quantities):
        for g in range(quantities // 3):
            for k, (one, other) in enumerate(rest_pairs()):
                c, q = one // 3, 3 * g + one % 3
                value = jnp.broadcast_to(star_ref[p, q, c : c + 1], (8, n))
                if other is not None:
                    c, q = other // 3, 3 * g + other % 3
                    value = jnp.where(lower, value, jnp.broadcast_to(star_ref[p, q, c : c + 1], (8, n)))
                out_ref[p, g * 5 + k] = value


def stacked(ref, first, count):
    return jnp.concatenate([ref[first + i] for i in range(count)], axis=0)


def star_mix(star_ref, rest_ref, t_ref, lane, quantities):
    within = lane if t_ref.shape[2] > LANES else pl.ds(0, LANES)
    acc, tails = [None] * quantities, [None] * quantities
    for g in range(quantities // 3):
        for k in range(9):
            t = t_ref[g, k * MAIN : (k + 1) * MAIN, within]
            c, q = k // 3, 3 * g + k % 3
            for p in range(quantities):
                term = jnp.broadcast_to(star_ref[p, q, c : c + 1, lane], (MAIN, LANES)) * t
                acc[p] = term if acc[p] is None else acc[p] + term
        for k in range(5):
            start = 9 * MAIN + 8 * k
            t = t_ref[g, start : start + 8, within]
            for p in range(quantities):
                term = rest_ref[p, g * 5 + k, :, lane] * t
                tails[p] = term if tails[p] is None else tails[p] + term
    return [
        jnp.concatenate([a, tail + pltpu.roll(tail, 4, 0)], axis=0) for a, tail in zip(acc, tails)
    ]


def lane_tiles(n, body):
    def one(tile, carry):
        body(pl.ds(pl.multiple_of(tile * LANES, LANES), LANES))
        return carry

    lax.fori_loop(0, n // LANES, one, 0)


def stiff_products(w_ref, v_ref, t_ref):
    for g in range(v_ref.shape[0] // 3):
        t_ref[g] = jnp.dot(w_ref[...], triple(stacked(v_ref, 3 * g, 3)), preferred_element_type=f32)


def series(w_ref, v_refs, t_refs, star_ref, rest_ref, sums, ready=lambda: None):
    quantities = v_refs[0].shape[0]
    lanes = [pl.ds(i * LANES, LANES) for i in range(len(v_refs))]
    for v_ref, t_ref, lane in zip(v_refs, t_refs, lanes):
        for ref, weights in sums:
            for q in range(quantities):
                ref[q, :, lane] = weights[0] * v_ref[q]
        stiff_products(w_ref, v_ref, t_ref)
    ready()

    def step(degree, last):
        def weight(weights):
            if last:
                return weights[3]
            return jnp.where(degree == 0, weights[1], weights[2])

        for v_ref, t_ref, lane in zip(v_refs, t_refs, lanes):
            acc = star_mix(star_ref, rest_ref, t_ref, lane, quantities)
            for p in range(quantities):
                value = -acc[p]
                if not last:
                    v_ref[p] = value
                for ref, weights in sums:
                    ref[p, :, lane] += weight(weights) * value
            if not last:
                stiff_products(w_ref, v_ref, t_ref)

    def body(degree, carry):
        step(degree, False)
        return carry

    lax.fori_loop(0, 2, body, 0)
    step(2, True)


def pack_sends(buffer_ref, lists_ref, out_refs, parity):
    quantities, rows, n = buffer_ref.shape
    high, low = split(stacked(buffer_ref, 0, quantities))
    both = jnp.concatenate([high, low], axis=0)
    count = lists_ref.shape[1]
    wanted = lists_ref[...]
    picks = []
    for e in range(DIRS):
        axis = e // 2
        even, odd = (1, 0) if e % 2 == 0 else (0, 1)
        row = jnp.where(
            parity[axis] == 0,
            wanted[2 * axis + even : 2 * axis + even + 1],
            wanted[2 * axis + odd : 2 * axis + odd + 1],
        )
        row = jnp.concatenate([row, jnp.full((1, LANES - count), -1, jnp.int32)], axis=1)
        picks.append((iota((n, LANES), 0) == row).astype(bf16))
    got = jnp.dot(both, jnp.concatenate(picks, axis=1), preferred_element_type=f32)
    total = got[: quantities * rows] + got[quantities * rows :]
    for e in range(DIRS):
        for q in range(quantities):
            out_refs[e][q] = total[q * rows : (q + 1) * rows, e * LANES : e * LANES + count]


def parities(axes):
    return [lax.rem(lax.axis_index(axis), 2) for axis in axes]


def predict_kernel(axes, *refs):
    sources, (stiff_ref, project_ref, lift_ref, sems), refs = refs[:12], refs[32:36], refs[12:32] + refs[36:]
    first_ref, late_ref, s0, s1, s2, s3, w_ref, wo_ref, wa_ref, wl_ref = refs[:10]
    kept, rest_ref, tiles = refs[10:19], refs[19], refs[20:]
    dofs_ref, star_ref, lists_ref = kept[:3]
    v_refs, t_refs = tiles[::2], tiles[1::2]
    h = step_length
    rows = first_ref.shape[1]
    targets = (stiff_ref, project_ref, lift_ref) + tuple(kept)
    copies = [pltpu.make_async_copy(src, dst, sems.at[i]) for i, (src, dst) in enumerate(zip(sources, targets))]
    for copy in copies:
        copy.start()
    for copy in copies[:3]:
        copy.wait()
    faces_basis = project_ref.shape[0]
    flat = jnp.concatenate([project_ref[b] for b in range(faces_basis)], axis=0)
    w_ref[...] = series_weights(stiff_ref, rows, False)
    height = w_ref.shape[0]
    wo_ref[:height] = series_weights(stiff_ref, rows, True)
    wo_ref[height:] = jnp.concatenate(block_weights(flat, rows, 3, False), axis=0).astype(bf16)
    wa_ref[...] = across_weights(project_ref)
    wl_ref[...] = lift_weights(lift_ref, rows)
    copies[3].wait()
    for q in range(dofs_ref.shape[0]):
        for i, v_ref in enumerate(v_refs):
            v_ref[q] = pad_rows(dofs_ref[q, :, i * LANES : (i + 1) * LANES], rows)
    sums = [(first_ref, weights_of(0.0, h)), (late_ref, weights_of(h, 2 * h))]
    def ready():
        copies[4].wait()
        rest_factors(star_ref, rest_ref)

    series(w_ref, v_refs, t_refs, star_ref, rest_ref, sums, ready)
    for copy in copies[5:]:
        copy.wait()
    pack_sends(first_ref, lists_ref, [s0, s1, s2, s3], parities(axes))


def effective(type_ref, near_ref, face_ref):
    kind = type_ref[...]
    n = kind.shape[1]
    index = jnp.where(kind == 0, near_ref[...], jnp.where(kind == 1, iota(kind.shape, 1), -1))
    source = jnp.where(kind == 0, face_ref[...], jnp.where(kind == 1, iota(kind.shape, 0), 0))
    return index, source


def across_weights(project_ref):
    faces_basis, faces, count = project_ref.shape
    main = (count // 8) * 8
    rest = count - main
    width = faces * count
    col = iota((count, 3 * width), 1) % width
    basis = jnp.where(col < faces * main, col % main, main + (col - faces * main) % rest)
    rep = (basis == iota((count, 3 * width), 0)).astype(bf16)
    tall = faces_basis * faces
    grow = (iota((tall, faces_basis), 0) // faces == iota((tall, faces_basis), 1)).astype(bf16)
    col = iota((tall, 3 * width), 1)
    inner = col % width
    owner = jnp.where(inner < faces * main, inner // main, (inner - faces * main) // rest)
    mine = owner == iota((tall, 3 * width), 0) % faces
    out = []
    for g in range(faces):
        matrix = jnp.concatenate([project_ref[b, g : g + 1] for b in range(faces_basis)], axis=0)
        high, low = spread(matrix, rep, False)
        high = jnp.dot(grow, high.astype(bf16), preferred_element_type=f32)
        low = jnp.dot(grow, low.astype(bf16), preferred_element_type=f32)
        out.append(jnp.where(mine, jnp.where(col < 2 * width, high, low), 0.0))
    return jnp.concatenate(out, axis=0).astype(bf16)


def across_operand(picked, q, rows, height):
    parts = []
    for part in range(2):
        start = part * height + q * rows
        main = [ref[start : start + 16] for ref in picked]
        rest = [ref[start + 16 : start + 24] for ref in picked]
        lower = iota(rest[0].shape, 0) < 4
        parts.append(
            jnp.concatenate(
                main + [jnp.where(lower, rest[0], rest[1]), jnp.where(lower, rest[2], rest[3])], axis=0
            )
        )
    return jnp.concatenate([parts[0], parts[1], parts[0]], axis=0).astype(bf16)


def across_traces(w_ref, picked, source, quantities, rows, store):
    height = quantities * rows
    faces = len(picked)
    tall = w_ref.shape[0] // faces
    wide = jnp.concatenate([source] * (tall // faces), axis=0)
    tests = [wide == g for g in range(faces - 1)]
    n = source.shape[1]
    for first in range(0, quantities, 2):
        group = range(first, min(first + 2, quantities))
        x = jnp.concatenate([across_operand(picked, q, rows, height) for q in group], axis=1)
        z = jnp.dot(w_ref[...], x, preferred_element_type=f32)
        for i, q in enumerate(group):
            mine = z[:, i * n : (i + 1) * n]
            value = mine[(faces - 1) * tall :]
            for g in reversed(range(faces - 1)):
                value = jnp.where(tests[g], mine[g * tall : (g + 1) * tall], value)
            store(q, value)


def flux_mix(flux_ref, trace_ref, lane, start):
    quantities, tall = trace_ref.shape[0], trace_ref.shape[1]
    faces = flux_ref.shape[2]
    acc = list(start)
    for q in range(quantities):
        t = trace_ref[q, :, lane]
        for p in range(quantities):
            factor = flux_ref[p, q, :, lane]
            term = jnp.concatenate([factor] * (tall // faces), axis=0) * t
            acc[p] = term if acc[p] is None else acc[p] + term
    return acc


def gather(operand, index, picked_ref, other_ref=None):
    faces, n = index.shape
    picks = [(iota((operand.shape[1], n), 0) == index[f : f + 1]).astype(bf16) for f in range(faces)]
    got = jnp.dot(operand, jnp.concatenate(picks, axis=1), preferred_element_type=f32)
    picked_ref[...] = got if other_ref is None else got + other_ref[...]
    return [picked_ref.at[:, f * n : (f + 1) * n] for f in range(faces)]


def own_kernel(own_ref, star_ref, rest_ref, minus_ref, w_ref, near_ref, face_ref, type_ref,
               part_ref, g_ref, picked_ref, trace_ref, t_ref):
    quantities, rows, n = own_ref.shape
    tall = trace_ref.shape[1]
    groups = quantities // 3
    x = jnp.concatenate([triple(stacked(own_ref, 3 * g, 3)) for g in range(groups)], axis=1)
    t = jnp.dot(w_ref[...], x, preferred_element_type=f32)
    height = t_ref.shape[1]
    for g in range(groups):
        t_ref[g] = t[:height, g * n : (g + 1) * n]
        for i in range(3):
            start = height + i * tall
            trace_ref[3 * g + i] = t[start : start + tall, g * n : (g + 1) * n]

    index, _ = effective(type_ref, near_ref, face_ref)
    high, low = split(stacked(own_ref, 0, quantities))
    gather(jnp.concatenate([high, low], axis=0), index, picked_ref)

    def tile(lane):
        acc = star_mix(star_ref, rest_ref, t_ref, lane, quantities)
        for p in range(quantities):
            part_ref[p, :, lane] = acc[p]
        acc = flux_mix(minus_ref, trace_ref, lane, [None] * quantities)
        for p in range(quantities):
            g_ref[p, :, lane] = acc[p]

    lane_tiles(n, tile)


def lift_weights(lift_ref, rows):
    faces_basis = lift_ref.shape[0]
    flat = jnp.concatenate([lift_ref[b] for b in range(faces_basis)], axis=0)
    blocks = block_weights(flat, flat.shape[0], 2, True)
    return jnp.concatenate([pad_rows(block, rows) for block in blocks], axis=0).astype(bf16)


def ghost_part(axes, got_refs, plus_ref, wa_ref, wl_ref, near_ref, face_ref, type_ref,
               part_ref, g_ref, own_picked_ref, picked_ref, trace_ref, flux_ref, emit):
    quantities, rows, n = part_ref.shape
    count = got_refs[0].shape[2]
    index, source = effective(type_ref, near_ref, face_ref)
    parity = parities(axes)
    ghost = index - n
    block = ghost // count
    axis_parity = jnp.where(block < 2, parity[0], parity[1])
    slot = (block // 2) * 2 + jnp.where(block % 2 == 1, axis_parity, 1 - axis_parity)
    column = jnp.where(ghost >= 0, slot * LANES + ghost % count, -1)
    operands = []
    for e in range(DIRS):
        high, low = split(stacked(got_refs[e], 0, quantities))
        both = jnp.concatenate([high, low], axis=0)
        empty = jnp.zeros((both.shape[0], LANES - count), bf16)
        operands.append(jnp.concatenate([both, empty], axis=1))
    picked = gather(jnp.concatenate(operands, axis=1), column, picked_ref, own_picked_ref)

    def keep(q, value):
        trace_ref[q] = value

    across_traces(wa_ref, picked, source, quantities, rows, keep)

    def tile(lane):
        acc = flux_mix(plus_ref, trace_ref, lane, [g_ref[p, :, lane] for p in range(quantities)])
        for p in range(quantities):
            flux_ref[p, :, lane] = acc[p]

    lane_tiles(n, tile)
    pairs = range(0, quantities, 2)
    operands = []
    for pair in pairs:
        other = flux_ref[pair + 1] if pair + 1 < quantities else jnp.zeros(flux_ref.shape[1:], f32)
        operands.append(triple(jnp.concatenate([flux_ref[pair], other], axis=0)))
    lifted = jnp.dot(wl_ref[...], jnp.concatenate(operands, axis=1), preferred_element_type=f32)
    for q in range(quantities):
        row, column = (q % 2) * rows, (q // 2) * n
        emit(q, part_ref[q] - lifted[row : row + rows, column : column + n])


def middle_kernel(axes, got0, got1, got2, got3, plus_ref, wa_ref, wl_ref, near_ref, face_ref, type_ref,
                  part_ref, g_ref, own_picked_ref, dofs_ref, star_ref, rest_ref, w_ref, cluster_ref, late_ref, lists_ref,
                  midway_ref, second_ref, s0, s1, s2, s3,
                  picked_ref, trace_ref, flux_ref, *tiles):
    v_refs, t_refs = tiles[::2], tiles[1::2]
    rows = part_ref.shape[1]
    quantities = part_ref.shape[0]

    def emit(q, change):
        value = pad_rows(dofs_ref[q], rows) + change
        midway_ref[q] = value
        for i, v_ref in enumerate(v_refs):
            v_ref[q] = value[:, i * LANES : (i + 1) * LANES]

    ghost_part(axes, [got0, got1, got2, got3], plus_ref, wa_ref, wl_ref, near_ref, face_ref, type_ref,
               part_ref, g_ref, own_picked_ref, picked_ref, trace_ref, flux_ref, emit)
    series(w_ref, v_refs, t_refs, star_ref, rest_ref, [(second_ref, weights_of(0.0, step_length))])
    fast = cluster_ref[...][None, :] == 0
    for q in range(quantities):
        second_ref[q] = jnp.where(fast, second_ref[q], late_ref[q])
    pack_sends(second_ref, lists_ref, [s0, s1, s2, s3], parities(axes))


def finish_kernel(axes, got0, got1, got2, got3, plus_ref, wa_ref, wl_ref, near_ref, face_ref, type_ref,
                  part_ref, g_ref, own_picked_ref, midway_ref, out_ref, picked_ref, trace_ref, flux_ref):
    count = out_ref.shape[1]

    def emit(q, change):
        out_ref[q] = (midway_ref[q] + change)[:count]

    ghost_part(axes, [got0, got1, got2, got3], plus_ref, wa_ref, wl_ref, near_ref, face_ref, type_ref,
               part_ref, g_ref, own_picked_ref, picked_ref, trace_ref, flux_ref, emit)


def call(kernel, name, args, outs, scratch, flops, far=(), vmem_bytes=20 << 20):
    spec = pl.BlockSpec(memory_space=pltpu.VMEM)
    hbm = pl.BlockSpec(memory_space=pltpu.HBM)
    size = sum(4 * math.prod(a.shape) for a in list(args) + list(outs))
    return pl.pallas_call(
        kernel,
        out_shape=[jax.ShapeDtypeStruct(s.shape, s.dtype) for s in outs],
        in_specs=[hbm if i in far else spec for i in range(len(args))],
        out_specs=[spec] * len(outs),
        scratch_shapes=scratch,
        cost_estimate=pl.CostEstimate(flops=flops, bytes_accessed=size, transcendentals=0),
        compiler_params=pltpu.CompilerParams(vmem_limit_bytes=vmem_bytes),
        name=name,
    )(*[pltpu.with_memory_space_constraint(a, pltpu.HBM) if i in far else a for i, a in enumerate(args)])


def exchange(block, axis, offset):
    count = lax.axis_size(axis)
    route = []
    for i in range(offset, count - 1, 2):
        route += [(i, i + 1), (i + 1, i)]
    return lax.ppermute(block, axis, route)


def swap(sends):
    return [
        exchange(sends[0], "px", 0),
        exchange(sends[1], "px", 1),
        exchange(sends[2], "py", 0),
        exchange(sends[3], "py", 1),
    ]


def per_device(dofs, star, flux_minus, flux_plus, stiffness, project, lift, cluster, neighbour, neighbour_face,
               face_type, send_list):
    axes = ("px", "py")
    quantities, count, n = dofs.shape
    faces, faces_basis = project.shape[:2]
    rows = 8 * pl.cdiv(count, 8)
    tall = faces * faces_basis
    width = send_list.shape[1]
    star = jnp.transpose(star, (1, 2, 0, 3))
    minus = jnp.transpose(flux_minus, (1, 2, 0, 3))
    plus = jnp.transpose(flux_plus, (1, 2, 0, 3))
    project = jnp.transpose(project, (1, 0, 2))
    lift = jnp.transpose(lift, (2, 0, 1))

    field = jax.ShapeDtypeStruct((quantities, rows, n), f32)
    traces = jax.ShapeDtypeStruct((quantities, tall, n), f32)
    sends = (jax.ShapeDtypeStruct((quantities, rows, width), f32),) * DIRS
    height = 9 * MAIN + 8 * len(rest_pairs())
    groups = quantities // 3
    weights = (
        jax.ShapeDtypeStruct((height, 9 * rows), bf16),
        jax.ShapeDtypeStruct((height + 3 * tall, 9 * rows), bf16),
        jax.ShapeDtypeStruct((faces * tall, 3 * faces * count), bf16),
        jax.ShapeDtypeStruct((2 * rows, 6 * tall), bf16),
    )
    tiles = [pltpu.VMEM((quantities, rows, LANES), f32), pltpu.VMEM((groups, height, LANES), f32)] * (n // LANES)
    t_field = pltpu.VMEM((groups, height, n), f32)
    t_trace = pltpu.VMEM((quantities, tall, n), f32)
    picked = pltpu.VMEM((2 * quantities * rows, faces * n), f32)

    local = (stiffness, project, lift)
    kept = (dofs, star, send_list, minus, plus, neighbour, neighbour_face, face_type, cluster)
    inputs = local + kept
    first, late, *out = call(
        functools.partial(predict_kernel, axes), "predict", inputs,
        (field, field, *sends, *weights, *(jax.ShapeDtypeStruct(a.shape, a.dtype) for a in kept),
         jax.ShapeDtypeStruct((quantities, groups * len(rest_pairs()), 8, n), f32)),
        [pltpu.VMEM(a.shape, a.dtype) for a in local] + [pltpu.SemaphoreType.DMA((len(inputs),))] + tiles,
        10_000_000, far=range(len(inputs)))
    out, (w, wo, wa, wl), kept = out[:DIRS], out[DIRS : 2 * DIRS], out[2 * DIRS :]
    dofs, star, send_list, minus, plus, neighbour, neighbour_face, face_type, cluster, rest = kept

    def own(buffer, name):
        return call(
            own_kernel, name, (buffer, star, rest, minus, wo, neighbour, neighbour_face, face_type),
            (field, traces, jax.ShapeDtypeStruct((2 * quantities * rows, faces * n), f32)),
            [t_trace, t_field], 10_000_000)

    ghost_scratch = [picked, t_trace, t_trace]
    got = swap(out)
    part, g, chosen = own(first, "own_first")
    midway, second, *out = call(
        functools.partial(middle_kernel, axes), "middle",
        (*got, plus, wa, wl, neighbour, neighbour_face, face_type, part, g, chosen, dofs, star, rest, w,
         cluster, late, send_list),
        (field, field, *sends),
        ghost_scratch + tiles, 10_000_000)
    got = swap(out)
    part, g, chosen = own(second, "own_second")
    (result,) = call(
        functools.partial(finish_kernel, axes), "finish",
        (*got, plus, wa, wl, neighbour, neighbour_face, face_type, part, g, chosen, midway),
        (jax.ShapeDtypeStruct((quantities, count, n), f32),), ghost_scratch, 10_000_000)
    return result


def solution(mesh):
    both = ("px", "py")
    in_specs = (
        P(None, None, both),
        P(None, None, None, both),
        P(None, None, None, both),
        P(None, None, None, both),
        P(),
        P(),
        P(),
        P(both),
        P(None, both),
        P(None, both),
        P(None, both),
        P(None, both),
    )
    return jax.shard_map(
        per_device, mesh=mesh, in_specs=in_specs, out_specs=P(None, None, both), check_vma=False
    )
```

```python
import functools
import math

import jax
import jax.numpy as jnp
from jax import lax
from jax.experimental import pallas as pl
from jax.experimental.pallas import tpu as pltpu
from jax.sharding import PartitionSpec as P

f32, bf16 = jnp.float32, jnp.bfloat16
step_length = 0.5
LANES = 128
DIRS = 4


def weights_of(lower, upper):
    return [
        (upper ** (m + 1) - lower ** (m + 1)) / math.factorial(m + 1) for m in range(4)
    ]


def iota(shape, dim):
    return lax.broadcasted_iota(jnp.int32, shape, dim)


def split(x):
    high = x.astype(bf16)
    return high, (x - high.astype(f32)).astype(bf16)


def triple(x):
    high = x.astype(bf16).astype(f32)
    return jnp.concatenate([high, x - high, high], axis=0).astype(bf16)


def pad_rows(x, rows):
    return jnp.concatenate([x, x[2 * x.shape[0] - rows :]], axis=0)


def spread(matrix, rep, transposed):
    dims = (((0,) if transposed else (1,), (0,)), ((), ()))
    high, low = split(matrix)
    return [
        lax.dot_general(part, rep, dims, preferred_element_type=f32)
        for part in (high, low)
    ]


def block_weights(matrix, inner, copies, transposed):
    count = matrix.shape[0] if transposed else matrix.shape[1]
    width = 3 * copies * inner
    rep = (iota((count, width), 1) % inner == iota((count, width), 0)).astype(bf16)
    high, low = spread(matrix, rep, transposed)
    col = iota(high.shape, 1)
    both = jnp.where(col < 2 * copies * inner, high, low)
    owner = (col % (copies * inner)) // inner
    return [jnp.where(owner == q, both, 0.0) for q in range(copies)]


MAIN = 16


def rest_pairs():
    return [(k, k + 1 if k + 1 < 9 else None) for k in range(0, 9, 2)]


def series_weights(stiff_ref, rows, transposed):
    blocks = []
    for c in range(3):
        blocks += block_weights(stiff_ref[c], rows, 3, transposed)
    out = [block[:MAIN] for block in blocks]
    for one, other in rest_pairs():
        tail = blocks[one][MAIN:]
        out += [tail, jnp.zeros_like(tail) if other is None else blocks[other][MAIN:]]
    return jnp.concatenate(out, axis=0).astype(bf16)


def rest_factors(star_ref, out_ref):
    quantities, _, _, n = star_ref.shape
    lower = iota((8, n), 0) < 4
    for p in range(quantities):
        for g in range(quantities // 3):
            for k, (one, other) in enumerate(rest_pairs()):
                c, q = one // 3, 3 * g + one % 3
                value = jnp.broadcast_to(star_ref[p, q, c : c + 1], (8, n))
                if other is not None:
                    c, q = other // 3, 3 * g + other % 3
                    value = jnp.where(lower, value, jnp.broadcast_to(star_ref[p, q, c : c + 1], (8, n)))
                out_ref[p, g * 5 + k] = value


def stacked(ref, first, count):
    return jnp.concatenate([ref[first + i] for i in range(count)], axis=0)


def star_mix(star_ref, rest_ref, t_ref, lane, quantities):
    within = lane if t_ref.shape[2] > LANES else pl.ds(0, LANES)
    acc, tails = [None] * quantities, [None] * quantities
    for g in range(quantities // 3):
        for k in range(9):
            t = t_ref[g, k * MAIN : (k + 1) * MAIN, within]
            c, q = k // 3, 3 * g + k % 3
            for p in range(quantities):
                term = jnp.broadcast_to(star_ref[p, q, c : c + 1, lane], (MAIN, LANES)) * t
                acc[p] = term if acc[p] is None else acc[p] + term
        for k in range(5):
            start = 9 * MAIN + 8 * k
            t = t_ref[g, start : start + 8, within]
            for p in range(quantities):
                term = rest_ref[p, g * 5 + k, :, lane] * t
                tails[p] = term if tails[p] is None else tails[p] + term
    return [
        jnp.concatenate([a, tail + pltpu.roll(tail, 4, 0)], axis=0) for a, tail in zip(acc, tails)
    ]


def lane_tiles(n, body):
    def one(tile, carry):
        body(pl.ds(pl.multiple_of(tile * LANES, LANES), LANES))
        return carry

    lax.fori_loop(0, n // LANES, one, 0)


def stiff_products(w_ref, v_ref, t_ref):
    for g in range(v_ref.shape[0] // 3):
        t_ref[g] = jnp.dot(w_ref[...], triple(stacked(v_ref, 3 * g, 3)), preferred_element_type=f32)


def series(w_ref, v_refs, t_refs, star_ref, rest_ref, sums, ready=lambda: None):
    quantities = v_refs[0].shape[0]
    lanes = [pl.ds(i * LANES, LANES) for i in range(len(v_refs))]
    for v_ref, t_ref, lane in zip(v_refs, t_refs, lanes):
        for ref, weights in sums:
            for q in range(quantities):
                ref[q, :, lane] = weights[0] * v_ref[q]
        stiff_products(w_ref, v_ref, t_ref)
    ready()

    def step(degree, last):
        def weight(weights):
            if last:
                return weights[3]
            return jnp.where(degree == 0, weights[1], weights[2])

        for v_ref, t_ref, lane in zip(v_refs, t_refs, lanes):
            acc = star_mix(star_ref, rest_ref, t_ref, lane, quantities)
            for p in range(quantities):
                value = -acc[p]
                if not last:
                    v_ref[p] = value
                for ref, weights in sums:
                    ref[p, :, lane] += weight(weights) * value
            if not last:
                stiff_products(w_ref, v_ref, t_ref)

    def body(degree, carry):
        step(degree, False)
        return carry

    lax.fori_loop(0, 2, body, 0)
    step(2, True)


def pack_sends(buffer_ref, lists_ref, out_refs, parity):
    quantities, rows, n = buffer_ref.shape
    high, low = split(stacked(buffer_ref, 0, quantities))
    both = jnp.concatenate([high, low], axis=0)
    count = lists_ref.shape[1]
    wanted = lists_ref[...]
    picks = []
    for e in range(DIRS):
        axis = e // 2
        even, odd = (1, 0) if e % 2 == 0 else (0, 1)
        row = jnp.where(
            parity[axis] == 0,
            wanted[2 * axis + even : 2 * axis + even + 1],
            wanted[2 * axis + odd : 2 * axis + odd + 1],
        )
        row = jnp.concatenate([row, jnp.full((1, LANES - count), -1, jnp.int32)], axis=1)
        picks.append((iota((n, LANES), 0) == row).astype(bf16))
    got = jnp.dot(both, jnp.concatenate(picks, axis=1), preferred_element_type=f32)
    total = got[: quantities * rows] + got[quantities * rows :]
    for e in range(DIRS):
        for q in range(quantities):
            out_refs[e][q] = total[q * rows : (q + 1) * rows, e * LANES : e * LANES + count]


def parities(axes):
    return [lax.rem(lax.axis_index(axis), 2) for axis in axes]


def predict_kernel(axes, *refs):
    sources, (stiff_ref, sems), refs = refs[:12], refs[32:34], refs[12:32] + refs[34:]
    first_ref, late_ref, s0, s1, s2, s3, w_ref, wo_ref = refs[:8]
    kept, rest_ref, tiles = refs[8:19], refs[19], refs[20:]
    project_ref, _, dofs_ref, star_ref, lists_ref = kept[:5]
    v_refs, t_refs = tiles[::2], tiles[1::2]
    h = step_length
    rows = first_ref.shape[1]
    targets = (stiff_ref,) + tuple(kept)
    copies = [pltpu.make_async_copy(src, dst, sems.at[i]) for i, (src, dst) in enumerate(zip(sources, targets))]
    for copy in copies:
        copy.start()
    for copy in copies[:3]:
        copy.wait()
    faces_basis = project_ref.shape[0]
    flat = jnp.concatenate([project_ref[b] for b in range(faces_basis)], axis=0)
    w_ref[...] = series_weights(stiff_ref, rows, False)
    height = w_ref.shape[0]
    wo_ref[:height] = series_weights(stiff_ref, rows, True)
    wo_ref[height:] = jnp.concatenate(block_weights(flat, rows, 3, False), axis=0).astype(bf16)
    copies[3].wait()
    for q in range(dofs_ref.shape[0]):
        for i, v_ref in enumerate(v_refs):
            v_ref[q] = pad_rows(dofs_ref[q, :, i * LANES : (i + 1) * LANES], rows)
    sums = [(first_ref, weights_of(0.0, h)), (late_ref, weights_of(h, 2 * h))]
    def ready():
        copies[4].wait()
        rest_factors(star_ref, rest_ref)

    series(w_ref, v_refs, t_refs, star_ref, rest_ref, sums, ready)
    for copy in copies[5:]:
        copy.wait()
    pack_sends(first_ref, lists_ref, [s0, s1, s2, s3], parities(axes))


def effective(type_ref, near_ref, face_ref):
    kind = type_ref[...]
    n = kind.shape[1]
    index = jnp.where(kind == 0, near_ref[...], jnp.where(kind == 1, iota(kind.shape, 1), -1))
    source = jnp.where(kind == 0, face_ref[...], jnp.where(kind == 1, iota(kind.shape, 0), 0))
    return index, source


def across_weights(project_ref):
    faces_basis, faces, count = project_ref.shape
    main = (count // 8) * 8
    rest = count - main
    width = faces * count
    col = iota((count, 3 * width), 1) % width
    basis = jnp.where(col < faces * main, col % main, main + (col - faces * main) % rest)
    rep = (basis == iota((count, 3 * width), 0)).astype(bf16)
    tall = faces_basis * faces
    grow = (iota((tall, faces_basis), 0) // faces == iota((tall, faces_basis), 1)).astype(bf16)
    col = iota((tall, 3 * width), 1)
    inner = col % width
    owner = jnp.where(inner < faces * main, inner // main, (inner - faces * main) // rest)
    mine = owner == iota((tall, 3 * width), 0) % faces
    out = []
    for g in range(faces):
        matrix = jnp.concatenate([project_ref[b, g : g + 1] for b in range(faces_basis)], axis=0)
        high, low = spread(matrix, rep, False)
        high = jnp.dot(grow, high.astype(bf16), preferred_element_type=f32)
        low = jnp.dot(grow, low.astype(bf16), preferred_element_type=f32)
        out.append(jnp.where(mine, jnp.where(col < 2 * width, high, low), 0.0))
    return jnp.concatenate(out, axis=0).astype(bf16)


def across_operand(picked, q, rows, height):
    parts = []
    for part in range(2):
        start = part * height + q * rows
        main = [ref[start : start + 16] for ref in picked]
        rest = [ref[start + 16 : start + 24] for ref in picked]
        lower = iota(rest[0].shape, 0) < 4
        parts.append(
            jnp.concatenate(
                main + [jnp.where(lower, rest[0], rest[1]), jnp.where(lower, rest[2], rest[3])], axis=0
            )
        )
    return jnp.concatenate([parts[0], parts[1], parts[0]], axis=0).astype(bf16)


def across_traces(w_ref, picked, source, quantities, rows, store):
    height = quantities * rows
    faces = len(picked)
    tall = w_ref.shape[0] // faces
    wide = jnp.concatenate([source] * (tall // faces), axis=0)
    tests = [wide == g for g in range(faces - 1)]
    n = source.shape[1]
    for first in range(0, quantities, 2):
        group = range(first, min(first + 2, quantities))
        x = jnp.concatenate([across_operand(picked, q, rows, height) for q in group], axis=1)
        z = jnp.dot(w_ref[...], x, preferred_element_type=f32)
        for i, q in enumerate(group):
            mine = z[:, i * n : (i + 1) * n]
            value = mine[(faces - 1) * tall :]
            for g in reversed(range(faces - 1)):
                value = jnp.where(tests[g], mine[g * tall : (g + 1) * tall], value)
            store(q, value)


def flux_mix(flux_ref, trace_ref, lane, start):
    quantities, tall = trace_ref.shape[0], trace_ref.shape[1]
    faces = flux_ref.shape[2]
    acc = list(start)
    for q in range(quantities):
        t = trace_ref[q, :, lane]
        for p in range(quantities):
            factor = flux_ref[p, q, :, lane]
            term = jnp.concatenate([factor] * (tall // faces), axis=0) * t
            acc[p] = term if acc[p] is None else acc[p] + term
    return acc


def gather(operand, index, picked_ref, other_ref=None):
    faces, n = index.shape
    picks = [(iota((operand.shape[1], n), 0) == index[f : f + 1]).astype(bf16) for f in range(faces)]
    got = jnp.dot(operand, jnp.concatenate(picks, axis=1), preferred_element_type=f32)
    picked_ref[...] = got if other_ref is None else got + other_ref[...]
    return [picked_ref.at[:, f * n : (f + 1) * n] for f in range(faces)]


def own_kernel(own_ref, star_ref, rest_ref, minus_ref, w_ref, near_ref, face_ref, type_ref, *refs):
    if len(refs) > 5:
        project_ref, lift_ref, part_ref, g_ref, picked_ref, wa_ref, wl_ref, trace_ref, t_ref = refs
        wa_ref[...] = across_weights(project_ref)
        wl_ref[...] = lift_weights(lift_ref, own_ref.shape[1])
    else:
        part_ref, g_ref, picked_ref, trace_ref, t_ref = refs
    quantities, rows, n = own_ref.shape
    tall = trace_ref.shape[1]
    groups = quantities // 3
    x = jnp.concatenate([triple(stacked(own_ref, 3 * g, 3)) for g in range(groups)], axis=1)
    t = jnp.dot(w_ref[...], x, preferred_element_type=f32)
    height = t_ref.shape[1]
    for g in range(groups):
        t_ref[g] = t[:height, g * n : (g + 1) * n]
        for i in range(3):
            start = height + i * tall
            trace_ref[3 * g + i] = t[start : start + tall, g * n : (g + 1) * n]

    index, _ = effective(type_ref, near_ref, face_ref)
    high, low = split(stacked(own_ref, 0, quantities))
    gather(jnp.concatenate([high, low], axis=0), index, picked_ref)

    def tile(lane):
        acc = star_mix(star_ref, rest_ref, t_ref, lane, quantities)
        for p in range(quantities):
            part_ref[p, :, lane] = acc[p]
        acc = flux_mix(minus_ref, trace_ref, lane, [None] * quantities)
        for p in range(quantities):
            g_ref[p, :, lane] = acc[p]

    lane_tiles(n, tile)


def lift_weights(lift_ref, rows):
    faces_basis = lift_ref.shape[0]
    flat = jnp.concatenate([lift_ref[b] for b in range(faces_basis)], axis=0)
    blocks = block_weights(flat, flat.shape[0], 2, True)
    return jnp.concatenate([pad_rows(block, rows) for block in blocks], axis=0).astype(bf16)


def ghost_part(axes, got_refs, plus_ref, wa_ref, wl_ref, near_ref, face_ref, type_ref,
               part_ref, g_ref, own_picked_ref, picked_ref, trace_ref, flux_ref, emit):
    quantities, rows, n = part_ref.shape
    count = got_refs[0].shape[2]
    index, source = effective(type_ref, near_ref, face_ref)
    parity = parities(axes)
    ghost = index - n
    block = ghost // count
    axis_parity = jnp.where(block < 2, parity[0], parity[1])
    slot = (block // 2) * 2 + jnp.where(block % 2 == 1, axis_parity, 1 - axis_parity)
    column = jnp.where(ghost >= 0, slot * LANES + ghost % count, -1)
    operands = []
    for e in range(DIRS):
        high, low = split(stacked(got_refs[e], 0, quantities))
        both = jnp.concatenate([high, low], axis=0)
        empty = jnp.zeros((both.shape[0], LANES - count), bf16)
        operands.append(jnp.concatenate([both, empty], axis=1))
    picked = gather(jnp.concatenate(operands, axis=1), column, picked_ref, own_picked_ref)

    def keep(q, value):
        trace_ref[q] = value

    across_traces(wa_ref, picked, source, quantities, rows, keep)

    def tile(lane):
        acc = flux_mix(plus_ref, trace_ref, lane, [g_ref[p, :, lane] for p in range(quantities)])
        for p in range(quantities):
            flux_ref[p, :, lane] = acc[p]

    lane_tiles(n, tile)
    pairs = range(0, quantities, 2)
    operands = []
    for pair in pairs:
        other = flux_ref[pair + 1] if pair + 1 < quantities else jnp.zeros(flux_ref.shape[1:], f32)
        operands.append(triple(jnp.concatenate([flux_ref[pair], other], axis=0)))
    lifted = jnp.dot(wl_ref[...], jnp.concatenate(operands, axis=1), preferred_element_type=f32)
    for q in range(quantities):
        row, column = (q % 2) * rows, (q // 2) * n
        emit(q, part_ref[q] - lifted[row : row + rows, column : column + n])


def middle_kernel(axes, got0, got1, got2, got3, plus_ref, wa_ref, wl_ref, near_ref, face_ref, type_ref,
                  part_ref, g_ref, own_picked_ref, dofs_ref, star_ref, rest_ref, w_ref, cluster_ref, late_ref, lists_ref,
                  midway_ref, second_ref, s0, s1, s2, s3,
                  picked_ref, trace_ref, flux_ref, *tiles):
    v_refs, t_refs = tiles[::2], tiles[1::2]
    rows = part_ref.shape[1]
    quantities = part_ref.shape[0]

    def emit(q, change):
        value = pad_rows(dofs_ref[q], rows) + change
        midway_ref[q] = value
        for i, v_ref in enumerate(v_refs):
            v_ref[q] = value[:, i * LANES : (i + 1) * LANES]

    ghost_part(axes, [got0, got1, got2, got3], plus_ref, wa_ref, wl_ref, near_ref, face_ref, type_ref,
               part_ref, g_ref, own_picked_ref, picked_ref, trace_ref, flux_ref, emit)
    series(w_ref, v_refs, t_refs, star_ref, rest_ref, [(second_ref, weights_of(0.0, step_length))])
    fast = cluster_ref[...][None, :] == 0
    for q in range(quantities):
        second_ref[q] = jnp.where(fast, second_ref[q], late_ref[q])
    pack_sends(second_ref, lists_ref, [s0, s1, s2, s3], parities(axes))


def finish_kernel(axes, got0, got1, got2, got3, plus_ref, wa_ref, wl_ref, near_ref, face_ref, type_ref,
                  part_ref, g_ref, own_picked_ref, midway_ref, out_ref, picked_ref, trace_ref, flux_ref):
    count = out_ref.shape[1]

    def emit(q, change):
        out_ref[q] = (midway_ref[q] + change)[:count]

    ghost_part(axes, [got0, got1, got2, got3], plus_ref, wa_ref, wl_ref, near_ref, face_ref, type_ref,
               part_ref, g_ref, own_picked_ref, picked_ref, trace_ref, flux_ref, emit)


def call(kernel, name, args, outs, scratch, flops, far=(), vmem_bytes=20 << 20):
    spec = pl.BlockSpec(memory_space=pltpu.VMEM)
    hbm = pl.BlockSpec(memory_space=pltpu.HBM)
    size = sum(4 * math.prod(a.shape) for a in list(args) + list(outs))
    return pl.pallas_call(
        kernel,
        out_shape=[jax.ShapeDtypeStruct(s.shape, s.dtype) for s in outs],
        in_specs=[hbm if i in far else spec for i in range(len(args))],
        out_specs=[spec] * len(outs),
        scratch_shapes=scratch,
        cost_estimate=pl.CostEstimate(flops=flops, bytes_accessed=size, transcendentals=0),
        compiler_params=pltpu.CompilerParams(vmem_limit_bytes=vmem_bytes),
        name=name,
    )(*[pltpu.with_memory_space_constraint(a, pltpu.HBM) if i in far else a for i, a in enumerate(args)])


def exchange(block, axis, offset):
    count = lax.axis_size(axis)
    route = []
    for i in range(offset, count - 1, 2):
        route += [(i, i + 1), (i + 1, i)]
    return lax.ppermute(block, axis, route)


def swap(sends):
    return [
        exchange(sends[0], "px", 0),
        exchange(sends[1], "px", 1),
        exchange(sends[2], "py", 0),
        exchange(sends[3], "py", 1),
    ]


def per_device(dofs, star, flux_minus, flux_plus, stiffness, project, lift, cluster, neighbour, neighbour_face,
               face_type, send_list):
    axes = ("px", "py")
    quantities, count, n = dofs.shape
    faces, faces_basis = project.shape[:2]
    rows = 8 * pl.cdiv(count, 8)
    tall = faces * faces_basis
    width = send_list.shape[1]
    star = jnp.transpose(star, (1, 2, 0, 3))
    minus = jnp.transpose(flux_minus, (1, 2, 0, 3))
    plus = jnp.transpose(flux_plus, (1, 2, 0, 3))
    project = jnp.transpose(project, (1, 0, 2))
    lift = jnp.transpose(lift, (2, 0, 1))

    field = jax.ShapeDtypeStruct((quantities, rows, n), f32)
    traces = jax.ShapeDtypeStruct((quantities, tall, n), f32)
    sends = (jax.ShapeDtypeStruct((quantities, rows, width), f32),) * DIRS
    height = 9 * MAIN + 8 * len(rest_pairs())
    groups = quantities // 3
    weights = (
        jax.ShapeDtypeStruct((height, 9 * rows), bf16),
        jax.ShapeDtypeStruct((height + 3 * tall, 9 * rows), bf16),
        jax.ShapeDtypeStruct((faces * tall, 3 * faces * count), bf16),
        jax.ShapeDtypeStruct((2 * rows, 6 * tall), bf16),
    )
    tiles = [pltpu.VMEM((quantities, rows, LANES), f32), pltpu.VMEM((groups, height, LANES), f32)] * (n // LANES)
    t_field = pltpu.VMEM((groups, height, n), f32)
    t_trace = pltpu.VMEM((quantities, tall, n), f32)
    picked = pltpu.VMEM((2 * quantities * rows, faces * n), f32)

    local = (stiffness,)
    kept = (project, lift, dofs, star, send_list, minus, plus, neighbour, neighbour_face, face_type, cluster)
    inputs = local + kept
    first, late, *out = call(
        functools.partial(predict_kernel, axes), "predict", inputs,
        (field, field, *sends, *weights[:2], *(jax.ShapeDtypeStruct(a.shape, a.dtype) for a in kept),
         jax.ShapeDtypeStruct((quantities, groups * len(rest_pairs()), 8, n), f32)),
        [pltpu.VMEM(a.shape, a.dtype) for a in local] + [pltpu.SemaphoreType.DMA((len(inputs),))] + tiles,
        10_000_000, far=range(len(inputs)))
    out, (w, wo), kept = out[:DIRS], out[DIRS : DIRS + 2], out[DIRS + 2 :]
    project, lift, dofs, star, send_list, minus, plus, neighbour, neighbour_face, face_type, cluster, rest = kept

    def own(buffer, name, more=(), made=()):
        return call(
            own_kernel, name, (buffer, star, rest, minus, wo, neighbour, neighbour_face, face_type, *more),
            (field, traces, jax.ShapeDtypeStruct((2 * quantities * rows, faces * n), f32), *made),
            [t_trace, t_field], 10_000_000)

    ghost_scratch = [picked, t_trace, t_trace]
    got = swap(out)
    part, g, chosen, wa, wl = own(first, "own_first", (project, lift), weights[2:])
    midway, second, *out = call(
        functools.partial(middle_kernel, axes), "middle",
        (*got, plus, wa, wl, neighbour, neighbour_face, face_type, part, g, chosen, dofs, star, rest, w,
         cluster, late, send_list),
        (field, field, *sends),
        ghost_scratch + tiles, 10_000_000)
    got = swap(out)
    part, g, chosen = own(second, "own_second")
    (result,) = call(
        functools.partial(finish_kernel, axes), "finish",
        (*got, plus, wa, wl, neighbour, neighbour_face, face_type, part, g, chosen, midway),
        (jax.ShapeDtypeStruct((quantities, count, n), f32),), ghost_scratch, 10_000_000)
    return result


def solution(mesh):
    both = ("px", "py")
    in_specs = (
        P(None, None, both),
        P(None, None, None, both),
        P(None, None, None, both),
        P(None, None, None, both),
        P(),
        P(),
        P(),
        P(both),
        P(None, both),
        P(None, both),
        P(None, both),
        P(None, both),
    )
    return jax.shard_map(
        per_device, mesh=mesh, in_specs=in_specs, out_specs=P(None, None, both), check_vma=False
    )
```
